512 devices in a mesh: dp: 64 (over y, x, core), mp: 8 (over z).
Axes of the slice: x: 4, y: 8, z: 8, core: 2. Of those that a mesh axis runs over, the one named last changes fastest.
Arguments:
- tokens: bfloat16 [65536, 2048], P('dp', 'mp'), may hold values from -6 to 6
- q_weight: bfloat16 [2048, 2048], P(None, 'mp'), may hold values from -0.125 to 0.125
- snippet_keys: bfloat16 [2048, 16, 2048], P('dp', None, 'mp'), may hold values from -500 to 500
- snippet_values: bfloat16 [2048, 16, 2048], P('dp', None, 'mp'), may hold values from -6 to 6
- out_cotangent: bfloat16 [65536, 2048], P('dp', 'mp'), may hold values from -6 to 6
- neighbour_ids: int32 [1024, 2], P('dp'), may hold values from 0 to 2047, as said below
- snippet_slot: int32 [2048], replicated, may hold values from 0 to 2047, as said below
Outputs:
- attended: bfloat16 [65536, 2048], P('dp', 'mp')
- input_grad: bfloat16 [65536, 2048], P('dp', 'mp')
- key_grad: float32 [2048, 16, 2048], P('dp', None, 'mp')
- value_grad: float32 [2048, 16, 2048], P('dp', None, 'mp')
The draws below stay inside these ranges and needn't reach their ends.
Inputs may be any that keep to these rules, and one draw needn't show every extreme that they name: A permutation: snippet s lies at global row snippet_slot[s] of snippet_keys and snippet_values, that is on dp index snippet_slot[s] // 32. `neighbour_ids`: the 32 neighbours named by the spans of one dp index are distinct snippets; at most 1 of them are stored on any one dp index, and exactly 1 on some.
All inputs are finite; a program needn't handle non-finite values.
Results may differ from the reference program's by a relative error of at most 0.022.
The reference program's roundings to bfloat16 on the way (of `queries`, `bf_weights`, `score_grad` and `query_grads`) count: a program that leaves them out, or rounds other values in their place, can miss the bound.
Values may be sent and summed in bfloat16 or wider, within the bound.
No kernel may reach another device: no remote copies, remote signals or barrier semaphores. Data moves between devices by JAX's collectives and lax.ppermute only.
A program may use at most 64 MiB of HBM per device.

```python
import math
import jax
import jax.numpy as jnp
from jax import lax

D = 2048
HEADS = 16
DH = 128
SPAN = 64
NEIGH = 2
NEI_LEN = 16
LEN = 1024
SNIP_DEV = 32
TOKENS = 65536
SNIPPETS = 2048
N_DP = 64
N_MP = 8


def neighbour_layout(key):
    table_key = jax.random.fold_in(key, 11)
    slot_table = jax.random.permutation(table_key, SNIPPETS).astype(jnp.int32)
    at_slot = jnp.zeros((SNIPPETS,), jnp.int32).at[slot_table].set(jnp.arange(SNIPPETS, dtype=jnp.int32))
    pick_total = NEIGH * (LEN // SPAN)
    pick_index = jnp.arange(pick_total, dtype=jnp.int32)
    owner_pos = pick_index % N_DP
    offset = pick_index // N_DP

    def one_device(device):
        device_key = jax.random.fold_in(jax.random.fold_in(key, 12), device)
        owner_order = jax.random.permutation(jax.random.fold_in(device_key, 1), N_DP).astype(jnp.int32)
        base_rows = jax.random.randint(jax.random.fold_in(device_key, 2), (N_DP,), 0, SNIP_DEV, dtype=jnp.int32)
        owners = owner_order[owner_pos]
        row_ids = (base_rows[owner_pos] + offset) % SNIP_DEV
        chosen = at_slot[owners * SNIP_DEV + row_ids]
        shuffle_order = jax.random.permutation(jax.random.fold_in(device_key, 3), pick_total)
        return chosen[shuffle_order].reshape(LEN // SPAN, NEIGH)
    per_device = jax.vmap(one_device)(jnp.arange(N_DP, dtype=jnp.int32))
    return (slot_table, per_device.reshape(N_DP * (LEN // SPAN), NEIGH).astype(jnp.int32))


def draw_snippet_slot(key, part):
    return neighbour_layout(key)[0]


def draw_neighbour_ids(key, part):
    return neighbour_layout(key)[1]


def draw_snippet_keys(key, part):
    normal_base = jnp.clip(jax.random.normal(jax.random.fold_in(key, 21), (SNIPPETS, NEI_LEN, D), jnp.float32), -6.0, 6.0)
    return normal_base.astype(jnp.bfloat16)


def level_of(key, dims, split, low, largest):
    def one(axis_at, parts):
        steps = jax.random.uniform(jax.random.fold_in(jax.random.fold_in(key, 6), axis_at), (parts,), jnp.float32, low / len(split), largest / len(split))
        return jnp.repeat(jnp.exp(steps), dims[axis_at] // parts).reshape((-1,) + (1,) * (len(dims) - axis_at - 1))

    factor_of = one(*split[0])
    for cut in split[1:]:
        factor_of = factor_of * one(*cut)
    return factor_of


def noise(own_key, dims, width, limit, shards=(), kind=jnp.bfloat16):
    gain = level_of(own_key, dims, shards, -0.22, 0.18) if shards else 1.0
    values = jax.random.normal(own_key, dims, jnp.float32) * width * gain
    return jnp.minimum(jnp.maximum(values, -limit), limit).astype(kind)


def setup_inputs(seed: int = 0) -> dict:
    arg_keys = jax.random.split(jax.random.key(seed), 8)
    return {
        "tokens": noise(arg_keys[0], (TOKENS, D), 1.0, 6.0, ((0, 64), (1, 8))),
        "q_weight": noise(arg_keys[1], (D, D), D ** -0.5, 0.125, ((1, 8),)),
        "snippet_keys": draw_snippet_keys(jax.random.fold_in(arg_keys[7], 71), 0),
        "snippet_values": noise(arg_keys[3], (SNIPPETS, NEI_LEN, D), 1.0, 6.0, ((0, 64), (2, 8))),
        "out_cotangent": noise(arg_keys[4], (TOKENS, D), 1.0, 6.0, ((0, 64), (1, 8))),
        "neighbour_ids": draw_neighbour_ids(jax.random.fold_in(arg_keys[7], 71), 0),
        "snippet_slot": draw_snippet_slot(jax.random.fold_in(arg_keys[7], 71), 0),
    }


def shift_in(matrix):
    columns = matrix.shape[-1]
    sequences = matrix.reshape(N_DP, LEN, columns)
    padding = jnp.zeros((N_DP, SPAN - 1, columns), matrix.dtype)
    moved = jnp.concatenate([sequences[:, SPAN - 1:], padding], axis=1)
    return moved.reshape(N_DP * (LEN // SPAN), SPAN, HEADS, DH)

def shift_out(blocks):
    sequences = blocks.reshape(N_DP, LEN, HEADS * DH)
    padding = jnp.zeros((N_DP, SPAN - 1, HEADS * DH), blocks.dtype)
    moved = jnp.concatenate([padding, sequences[:, :LEN - SPAN + 1]], axis=1)
    return moved.reshape(N_DP * LEN, HEADS * DH)

def reference(tokens, q_weight, snippet_keys, snippet_values, out_cotangent, neighbour_ids, snippet_slot):
    scaling = 1.0 / math.sqrt(DH)
    span_total = N_DP * (LEN // SPAN)
    queries = jnp.dot(tokens, q_weight, preferred_element_type=jnp.float32).astype(jnp.bfloat16)
    stored_rows = snippet_slot[neighbour_ids].astype(jnp.int32)
    key_blocks = snippet_keys[stored_rows].reshape(span_total, NEIGH * NEI_LEN, HEADS, DH).astype(jnp.float32)
    value_blocks = snippet_values[stored_rows].reshape(span_total, NEIGH * NEI_LEN, HEADS, DH).astype(jnp.float32)
    shifted_q = shift_in(queries).astype(jnp.float32)
    grad_rows = shift_in(out_cotangent).astype(jnp.float32)
    scores = jnp.einsum('cqhd,ckhd->chqk', shifted_q, key_blocks) * scaling
    row_max = lax.optimization_barrier(jnp.max(scores, axis=-1, keepdims=True))
    shifted_exp = jnp.exp(scores - row_max)
    weights = shifted_exp / lax.optimization_barrier(jnp.sum(shifted_exp, axis=-1, keepdims=True))
    bf_weights = lax.optimization_barrier(weights.astype(jnp.bfloat16)).astype(jnp.float32)
    attended = shift_out(jnp.einsum('chqk,ckhd->cqhd', bf_weights, value_blocks).astype(jnp.bfloat16))
    prob_grad = jnp.einsum('cqhd,ckhd->chqk', grad_rows, value_blocks)
    row_delta = lax.optimization_barrier(jnp.sum(weights * prob_grad, axis=-1, keepdims=True))
    score_grad = lax.optimization_barrier((weights * (prob_grad - row_delta)).astype(jnp.bfloat16)).astype(jnp.float32)
    query_grads = shift_out((jnp.einsum('chqk,ckhd->cqhd', score_grad, key_blocks) * scaling).astype(jnp.bfloat16))
    key_use = jnp.einsum('chqk,cqhd->ckhd', score_grad, shifted_q) * scaling
    value_use = jnp.einsum('chqk,cqhd->ckhd', bf_weights, grad_rows)
    flat_rows = stored_rows.reshape(-1)
    key_grad = jnp.zeros((SNIPPETS, NEI_LEN, D), jnp.float32).at[flat_rows].add(key_use.reshape(-1, NEI_LEN, D))
    value_grad = jnp.zeros((SNIPPETS, NEI_LEN, D), jnp.float32).at[flat_rows].add(value_use.reshape(-1, NEI_LEN, D))
    group_width = HEADS // N_MP * DH
    input_grad = jnp.zeros((TOKENS, D), jnp.float32)
    for group_index in range(N_MP):
        first_col = group_index * group_width
        last_col = first_col + group_width
        term = jnp.dot(query_grads[:, first_col:last_col], q_weight[:, first_col:last_col].T, preferred_element_type=jnp.float32)
        input_grad = input_grad + lax.optimization_barrier(term.astype(jnp.bfloat16)).astype(jnp.float32)
    return (attended, input_grad.astype(jnp.bfloat16), key_grad, value_grad)
```

```python
import math

import jax
import jax.numpy as jnp
from jax import lax
from jax.experimental import pallas as pl
from jax.experimental.pallas import tpu as pltpu
from jax.sharding import PartitionSpec as P

DH = 128
SPAN = 64
NEIGH = 2
TILE = 2 * SPAN
BLOCK = 2 * TILE
LANES = 128
F32 = jnp.float32
BF16 = jnp.bfloat16

VMEM = pl.BlockSpec(memory_space=pltpu.MemorySpace.VMEM)
SMEM = pl.BlockSpec(memory_space=pltpu.MemorySpace.SMEM)
HBM = pl.BlockSpec(memory_space=pltpu.MemorySpace.HBM)


def dot_nt(a, b):
    return lax.dot_general(a, b, (((1,), (1,)), ((), ())), preferred_element_type=F32)


def dot_tn(a, b):
    return lax.dot_general(a, b, (((0,), (0,)), ((), ())), preferred_element_type=F32)


def request_rows(ids, slot_table, snip_count, dp_count):
    spans = ids.shape[1]

    def kernel(ids_ref, slot_ref, req_ref, own_ref):
        def clear(i, c):
            req_ref[i, 0, 0] = 0
            return c

        lax.fori_loop(0, dp_count, clear, 0)

        def step(i, c):
            for n in range(NEIGH):
                slot = slot_ref[ids_ref[n, i]]
                owner = lax.div(slot, snip_count)
                req_ref[owner, 0, 0] = slot - owner * snip_count + 1
                own_ref[i * NEIGH + n] = owner
            return c

        lax.fori_loop(0, spans, step, 0)

    return pl.pallas_call(
        kernel,
        out_shape=(
            jax.ShapeDtypeStruct((dp_count, 1, LANES), jnp.int32),
            jax.ShapeDtypeStruct((spans * NEIGH,), jnp.int32),
        ),
        in_specs=[SMEM, SMEM],
        out_specs=(SMEM, SMEM),
        name="request_rows",
    )(ids, slot_table)


def pick_rows(wanted, keys, values):
    dp_count = wanted.shape[0]
    _, nei, width = keys.shape

    def kernel(want_ref, key_ref, value_ref, out_ref):
        def step(i, c):
            row = jnp.maximum(want_ref[i, 0, 0] - 1, 0)
            out_ref[i, :, :width] = key_ref[row]
            out_ref[i, :, width:] = value_ref[row]
            return c

        lax.fori_loop(0, dp_count, step, 0, unroll=4)

    return pl.pallas_call(
        kernel,
        out_shape=jax.ShapeDtypeStruct((dp_count, nei, 2 * width), keys.dtype),
        in_specs=[SMEM, VMEM, VMEM],
        out_specs=VMEM,
        name="pick_rows",
    )(wanted, keys, values)


def sum_uses(wanted, back, snip_count):
    dp_count, nei, twice = back.shape
    width = twice // 2

    def kernel(want_ref, back_ref, key_ref, value_ref):
        key_ref[...] = jnp.zeros_like(key_ref)
        value_ref[...] = jnp.zeros_like(value_ref)

        def step(i, c):
            want = want_ref[i, 0, 0]

            @pl.when(want > 0)
            def _():
                row = jnp.maximum(want - 1, 0)
                key_ref[row] += back_ref[i, :, :width].astype(F32)
                value_ref[row] += back_ref[i, :, width:].astype(F32)

            return c

        lax.fori_loop(0, dp_count, step, 0)

    out = jax.ShapeDtypeStruct((snip_count, nei, width), F32)
    return pl.pallas_call(
        kernel,
        out_shape=(out, out),
        in_specs=[SMEM, VMEM],
        out_specs=(VMEM, VMEM),
        name="sum_uses",
    )(wanted, back)


def attend(owners, tokens, q_weight, cotangent, got):
    seq_len, width = cotangent.shape
    mp_count = tokens.shape[0]
    dp_count, nei, _ = got.shape
    heads = width // DH
    picks = owners.shape[0]
    span_keys = NEIGH * nei
    tile_keys = 3 * span_keys
    blocks = seq_len // BLOCK
    scaling = 1.0 / math.sqrt(DH)

    def kernel(
        own_ref, tok_hbm, w_ref, cot_hbm, got_ref, att_ref, term_hbm, use_ref,
        tok_ref, cot_ref, term_ref, q_ref, qg_ref, k_ref, v_ref, ku_ref, vu_ref, in_sem, cot_sem, out_sem,
    ):
        def load(b):
            rows = slice(b * BLOCK, (b + 1) * BLOCK)
            return pltpu.make_async_copy(tok_hbm.at[:, rows, :], tok_ref.at[:, rows, :], in_sem.at[b])

        def store(b):
            rows = slice(b * BLOCK, (b + 1) * BLOCK)
            return pltpu.make_async_copy(term_ref.at[rows, :], term_hbm.at[rows, :], out_sem.at[b])

        load(0).start()
        load_cot = pltpu.make_async_copy(cot_hbm, cot_ref, cot_sem)
        load_cot.start()
        for b in range(1, blocks):
            load(b).start()
        k_ref[:span_keys, :] = jnp.zeros((span_keys, width), BF16)
        v_ref[:span_keys, :] = jnp.zeros((span_keys, width), BF16)
        for n in range(picks):
            at = span_keys + n * nei
            k_ref[at : at + nei, :] = got_ref[own_ref[n], :, :width]
            v_ref[at : at + nei, :] = got_ref[own_ref[n], :, width:]
        use_ref[...] = jnp.zeros_like(use_ref)
        key_at = lax.broadcasted_iota(jnp.int32, (tile_keys, TILE), 0) // span_keys
        span_of = (lax.broadcasted_iota(jnp.int32, (tile_keys, TILE), 1) + 1) // SPAN
        inner = key_at == span_of
        first_tile = inner & (key_at > 0)

        def one_tile(t):
            mask = inner if t else first_tile
            rows = slice(t * TILE, (t + 1) * TILE)
            start = t * NEIGH * span_keys
            keys_at = slice(start, start + tile_keys)
            for h in range(heads):
                cols = slice(h * DH, (h + 1) * DH)
                q = q_ref[rows, cols]
                cot = cot_ref[rows, cols]
                k = k_ref[keys_at, cols]
                v = v_ref[keys_at, cols]
                scores = jnp.where(mask, dot_nt(k, q) * scaling, -jnp.inf)
                top = jnp.max(scores, axis=0, keepdims=True)
                top = jnp.where(top == -jnp.inf, 0.0, top)
                grown = jnp.exp(scores - top)
                total = jnp.sum(grown, axis=0, keepdims=True)
                weights = grown * (1.0 / jnp.where(total > 0.0, total, 1.0))
                bf_weights = weights.astype(BF16)
                prob_grad = dot_nt(v, cot)
                row_delta = jnp.sum(weights * prob_grad, axis=0, keepdims=True)
                score_grad = (weights * (prob_grad - row_delta)).astype(BF16)
                att_ref[rows, cols] = dot_tn(bf_weights, v).astype(BF16)
                qg_ref[rows, cols] = (dot_tn(score_grad, k) * scaling).astype(BF16)
                key_use = jnp.dot(score_grad, q, preferred_element_type=F32)
                value_use = jnp.dot(bf_weights, cot, preferred_element_type=F32)
                mid, end = start + span_keys, start + tile_keys
                if t == 0:
                    ku_ref[start:mid, cols] = key_use[:span_keys]
                    vu_ref[start:mid, cols] = value_use[:span_keys]
                else:
                    ku_ref[start:mid, cols] += key_use[:span_keys]
                    vu_ref[start:mid, cols] += value_use[:span_keys]
                ku_ref[mid:end, cols] = key_use[span_keys:]
                vu_ref[mid:end, cols] = value_use[span_keys:]

        for b in range(blocks):
            rows = slice(b * BLOCK, (b + 1) * BLOCK)
            load(b).wait()
            acc = None
            for j in range(mp_count):
                w = w_ref[j * width : (j + 1) * width, :]
                x = jnp.dot(tok_ref[j, rows, :], w, preferred_element_type=F32)
                acc = x if acc is None else acc + x
            q_ref[rows, :] = acc.astype(BF16)
            if b == 0:
                load_cot.wait()
            for t in range(b * BLOCK // TILE, (b + 1) * BLOCK // TILE):
                one_tile(t)
            qg = qg_ref[rows, :]
            for j in range(mp_count):
                at = slice(j * width, (j + 1) * width)
                term_ref[rows, at] = dot_nt(qg, w_ref[at, :]).astype(BF16)
            store(b).start()
        for n in range(picks):
            at = span_keys + n * nei
            use_ref[own_ref[n], :, :width] = (ku_ref[at : at + nei, :] * scaling).astype(BF16)
            use_ref[own_ref[n], :, width:] = vu_ref[at : at + nei, :].astype(BF16)
        for b in range(blocks):
            store(b).wait()

    padded = (seq_len // SPAN + 1) * span_keys
    return pl.pallas_call(
        kernel,
        out_shape=(
            jax.ShapeDtypeStruct((seq_len, width), BF16),
            jax.ShapeDtypeStruct((seq_len, mp_count * width), BF16),
            jax.ShapeDtypeStruct((dp_count, nei, 2 * width), BF16),
        ),
        in_specs=[SMEM, HBM, VMEM, HBM, VMEM],
        out_specs=(VMEM, HBM, VMEM),
        scratch_shapes=[
            pltpu.VMEM((mp_count, seq_len, width), BF16),
            pltpu.VMEM((seq_len, width), BF16),
            pltpu.VMEM((seq_len, mp_count * width), BF16),
            pltpu.VMEM((seq_len, width), BF16),
            pltpu.VMEM((seq_len, width), BF16),
            pltpu.VMEM((padded, width), BF16),
            pltpu.VMEM((padded, width), BF16),
            pltpu.VMEM((padded, width), F32),
            pltpu.VMEM((padded, width), F32),
            pltpu.SemaphoreType.DMA((blocks,)),
            pltpu.SemaphoreType.DMA(()),
            pltpu.SemaphoreType.DMA((blocks,)),
        ],
        compiler_params=pltpu.CompilerParams(vmem_limit_bytes=24 * 1024 * 1024),
        name="attend",
    )(owners, tokens, q_weight, cotangent, got)


def body(
    tokens, q_weight, snippet_keys, snippet_values, out_cotangent, neighbour_ids, snippet_slot
):
    dp_count = lax.axis_size("dp")
    snip_count = snippet_keys.shape[0]
    gathered = lax.all_gather(tokens, "mp", axis=0, tiled=False)
    request, owners = request_rows(neighbour_ids.T, snippet_slot, snip_count, dp_count)
    wanted = lax.all_to_all(request, "dp", split_axis=0, concat_axis=0, tiled=True)
    picked = pick_rows(wanted, snippet_keys, snippet_values)
    got = lax.all_to_all(picked, "dp", split_axis=0, concat_axis=0, tiled=True)
    attended, terms, uses = attend(owners, gathered, q_weight, out_cotangent, got)
    input_grad = lax.psum_scatter(terms, "mp", scatter_dimension=1, tiled=True)
    back = lax.all_to_all(uses, "dp", split_axis=0, concat_axis=0, tiled=True)
    key_grad, value_grad = sum_uses(wanted, back, snip_count)
    return (attended, input_grad, key_grad, value_grad)


def solution(mesh):
    return jax.shard_map(
        body,
        mesh=mesh,
        in_specs=(
            P("dp", "mp"),
            P(None, "mp"),
            P("dp", None, "mp"),
            P("dp", None, "mp"),
            P("dp", "mp"),
            P("dp", None),
            P(),
        ),
        out_specs=(P("dp", "mp"), P("dp", "mp"), P("dp", None, "mp"), P("dp", None, "mp")),
        check_vma=False,
    )
```

```python
import math

import jax
import jax.numpy as jnp
from jax import lax
from jax.experimental import pallas as pl
from jax.experimental.pallas import tpu as pltpu
from jax.sharding import PartitionSpec as P

DH = 128
SPAN = 64
NEIGH = 2
TILE = 2 * SPAN
BLOCK = 2 * TILE
LANES = 128
F32 = jnp.float32
BF16 = jnp.bfloat16

VMEM = pl.BlockSpec(memory_space=pltpu.MemorySpace.VMEM)
SMEM = pl.BlockSpec(memory_space=pltpu.MemorySpace.SMEM)
HBM = pl.BlockSpec(memory_space=pltpu.MemorySpace.HBM)


def dot_nt(a, b):
    return lax.dot_general(a, b, (((1,), (1,)), ((), ())), preferred_element_type=F32)


def dot_tn(a, b):
    return lax.dot_general(a, b, (((0,), (0,)), ((), ())), preferred_element_type=F32)


def request_rows(ids, slot_table, snip_count, dp_count):
    spans = ids.shape[1]

    def kernel(ids_ref, slot_ref, req_ref, own_ref):
        def clear(i, c):
            req_ref[i, 0, 0] = 0
            return c

        lax.fori_loop(0, dp_count, clear, 0)

        def step(i, c):
            for n in range(NEIGH):
                slot = slot_ref[ids_ref[n, i]]
                owner = lax.div(slot, snip_count)
                req_ref[owner, 0, 0] = slot - owner * snip_count + 1
                own_ref[i * NEIGH + n] = owner
            return c

        lax.fori_loop(0, spans, step, 0)

    return pl.pallas_call(
        kernel,
        out_shape=(
            jax.ShapeDtypeStruct((dp_count, 1, LANES), jnp.int32),
            jax.ShapeDtypeStruct((spans * NEIGH,), jnp.int32),
        ),
        in_specs=[SMEM, SMEM],
        out_specs=(SMEM, SMEM),
        name="request_rows",
    )(ids, slot_table)


def pick_rows(wanted, keys, values):
    dp_count = wanted.shape[0]
    _, nei, width = keys.shape

    def kernel(want_ref, key_ref, value_ref, out_ref):
        def step(i, c):
            row = jnp.maximum(want_ref[i, 0, 0] - 1, 0)
            out_ref[i, :, :width] = key_ref[row]
            out_ref[i, :, width:] = value_ref[row]
            return c

        lax.fori_loop(0, dp_count, step, 0, unroll=4)

    return pl.pallas_call(
        kernel,
        out_shape=jax.ShapeDtypeStruct((dp_count, nei, 2 * width), keys.dtype),
        in_specs=[SMEM, VMEM, VMEM],
        out_specs=VMEM,
        name="pick_rows",
    )(wanted, keys, values)


def sum_uses(wanted, back, snip_count):
    dp_count, nei, twice = back.shape
    width = twice // 2

    def kernel(want_ref, back_ref, key_ref, value_ref):
        key_ref[...] = jnp.zeros_like(key_ref)
        value_ref[...] = jnp.zeros_like(value_ref)

        def step(i, c):
            want = want_ref[i, 0, 0]

            @pl.when(want > 0)
            def _():
                row = jnp.maximum(want - 1, 0)
                key_ref[row] += back_ref[i, :, :width].astype(F32)
                value_ref[row] += back_ref[i, :, width:].astype(F32)

            return c

        lax.fori_loop(0, dp_count, step, 0)

    out = jax.ShapeDtypeStruct((snip_count, nei, width), F32)
    return pl.pallas_call(
        kernel,
        out_shape=(out, out),
        in_specs=[SMEM, VMEM],
        out_specs=(VMEM, VMEM),
        name="sum_uses",
    )(wanted, back)


def attend(rows_at, owners, me, tokens, q_weight, cotangent, got, carried, ring):
    seq_len, width = cotangent.shape
    mp_count = tokens.shape[0]
    dp_count, nei, _ = got.shape
    heads = width // DH
    picks = owners.shape[0]
    span_keys = NEIGH * nei
    tile_keys = 3 * span_keys
    low, high = rows_at
    count = high - low
    blocks = count // BLOCK
    key_low = low // SPAN * span_keys
    key_rows = count // SPAN * span_keys + span_keys
    scaling = 1.0 / math.sqrt(DH)
    n_extra = len(carried)

    def kernel(own_ref, me_ref, tok_hbm, w_ref, cot_hbm, got_ref, *refs):
        carried_refs, refs = refs[:n_extra], refs[n_extra:]
        att_hbm = refs[0]
        if ring:
            use_ref, target_refs = refs[1], refs[2 : 2 + len(ring)]
            refs = refs[2 + len(ring) :]
            ku_ref, vu_ref = refs[-2:]
        else:
            term_hbm, ku_ref, vu_ref = refs[1:4]
            refs = refs[4:]
        tok_ref, cot_ref, att_ref, term_ref, q_ref, qg_ref, k_ref, v_ref = refs[:8]
        in_sem, cot_sem, att_sem, out_sem = refs[8:12]

        def load(b):
            rows = slice(b * BLOCK, (b + 1) * BLOCK)
            source = tok_hbm.at[:, slice(low + b * BLOCK, low + (b + 1) * BLOCK), :]
            return pltpu.make_async_copy(source, tok_ref.at[:, rows, :], in_sem.at[b])

        def store(b):
            rows = slice(b * BLOCK, (b + 1) * BLOCK)
            return pltpu.make_async_copy(term_ref.at[rows, :], term_hbm.at[rows, :], out_sem.at[b])

        load(0).start()
        load_cot = pltpu.make_async_copy(cot_hbm.at[low:high, :], cot_ref, cot_sem)
        load_cot.start()
        for b in range(1, blocks):
            load(b).start()
        if low == 0:
            k_ref[:span_keys, :] = jnp.zeros((span_keys, width), BF16)
            v_ref[:span_keys, :] = jnp.zeros((span_keys, width), BF16)
        for n in range(picks):
            at = span_keys + n * nei - key_low
            if 0 <= at < key_rows:
                k_ref[at : at + nei, :] = got_ref[own_ref[n], :, :width]
                v_ref[at : at + nei, :] = got_ref[own_ref[n], :, width:]
        key_at = lax.broadcasted_iota(jnp.int32, (tile_keys, TILE), 0) // span_keys
        span_of = (lax.broadcasted_iota(jnp.int32, (tile_keys, TILE), 1) + 1) // SPAN
        inner = key_at == span_of
        first_tile = inner & (key_at > 0)

        def one_tile(t):
            mask = first_tile if low == 0 and t == 0 else inner
            rows = slice(t * TILE, (t + 1) * TILE)
            start = t * NEIGH * span_keys
            keys_at = slice(start, start + tile_keys)
            for h in range(heads):
                cols = slice(h * DH, (h + 1) * DH)
                q = q_ref[rows, cols]
                cot = cot_ref[rows, cols]
                k = k_ref[keys_at, cols]
                v = v_ref[keys_at, cols]
                scores = jnp.where(mask, dot_nt(k, q) * scaling, -jnp.inf)
                top = jnp.max(scores, axis=0, keepdims=True)
                top = jnp.where(top == -jnp.inf, 0.0, top)
                grown = jnp.exp(scores - top)
                total = jnp.sum(grown, axis=0, keepdims=True)
                weights = grown * (1.0 / jnp.where(total > 0.0, total, 1.0))
                bf_weights = weights.astype(BF16)
                prob_grad = dot_nt(v, cot)
                row_delta = jnp.sum(weights * prob_grad, axis=0, keepdims=True)
                score_grad = (weights * (prob_grad - row_delta)).astype(BF16)
                att_ref[rows, cols] = dot_tn(bf_weights, v).astype(BF16)
                qg_ref[rows, cols] = (dot_tn(score_grad, k) * scaling).astype(BF16)
                key_use = jnp.dot(score_grad, q, preferred_element_type=F32)
                value_use = jnp.dot(bf_weights, cot, preferred_element_type=F32)
                mid, end = start + span_keys, start + tile_keys
                if t == 0:
                    ku_ref[start:mid, cols] = key_use[:span_keys]
                    vu_ref[start:mid, cols] = value_use[:span_keys]
                else:
                    ku_ref[start:mid, cols] += key_use[:span_keys]
                    vu_ref[start:mid, cols] += value_use[:span_keys]
                ku_ref[mid:end, cols] = key_use[span_keys:]
                vu_ref[mid:end, cols] = value_use[span_keys:]

        for b in range(blocks):
            rows = slice(b * BLOCK, (b + 1) * BLOCK)
            load(b).wait()
            acc = None
            for j in range(mp_count):
                w = w_ref[j * width : (j + 1) * width, :]
                x = jnp.dot(tok_ref[j, rows, :], w, preferred_element_type=F32)
                acc = x if acc is None else acc + x
            q_ref[rows, :] = acc.astype(BF16)
            if b == 0:
                load_cot.wait()
            for t in range(b * BLOCK // TILE, (b + 1) * BLOCK // TILE):
                one_tile(t)
            qg = qg_ref[rows, :]
            if not ring:
                for j in range(mp_count):
                    at = slice(j * width, (j + 1) * width)
                    term_ref[rows, at] = dot_nt(qg, w_ref[at, :]).astype(BF16)
                store(b).start()
            else:
                for (offset, first, size), ref in zip(ring, target_refs):
                    if first <= b * BLOCK < first + size:
                        target = lax.rem(me_ref[0] + offset, mp_count)
                        w = w_ref[pl.ds(pl.multiple_of(target * width, width), width), :]
                        at = slice(b * BLOCK - first, (b + 1) * BLOCK - first)
                        ref[at, :] = dot_nt(qg, w).astype(BF16)
        keep = pltpu.make_async_copy(att_ref, att_hbm.at[low:high, :], att_sem)
        keep.start()
        if ring:
            use_ref[...] = jnp.zeros_like(use_ref)
            earlier_ku, earlier_vu = carried_refs[1:]
            for n in range(picks):
                at = span_keys + n * nei
                key_use = value_use = None
                if at < low // SPAN * span_keys + span_keys:
                    key_use = earlier_ku[at : at + nei, :]
                    value_use = earlier_vu[at : at + nei, :]
                if at >= key_low:
                    mine = slice(at - key_low, at - key_low + nei)
                    key_use = ku_ref[mine, :] if key_use is None else key_use + ku_ref[mine, :]
                    value_use = vu_ref[mine, :] if value_use is None else value_use + vu_ref[mine, :]
                use_ref[own_ref[n], :, :width] = (key_use * scaling).astype(BF16)
                use_ref[own_ref[n], :, width:] = value_use.astype(BF16)
        else:
            for b in range(blocks):
                store(b).wait()
        keep.wait()

    sums = jax.ShapeDtypeStruct((key_rows, width), F32)
    whole = jax.ShapeDtypeStruct((seq_len, width), BF16)
    if ring:
        outs = [whole, jax.ShapeDtypeStruct((dp_count, nei, 2 * width), BF16)]
        outs += [jax.ShapeDtypeStruct((size, width), BF16) for _, _, size in ring]
        specs = [HBM] + [VMEM] * (len(ring) + 1)
        last = [pltpu.VMEM((key_rows, width), F32), pltpu.VMEM((key_rows, width), F32)]
        aliases = {6: 0}
    else:
        outs = [whole, jax.ShapeDtypeStruct((count, mp_count * width), BF16), sums, sums]
        specs = [HBM, HBM, VMEM, VMEM]
        last = []
        aliases = {}
    return pl.pallas_call(
        kernel,
        out_shape=tuple(outs),
        in_specs=[SMEM, SMEM, HBM, VMEM, HBM, VMEM] + ([HBM, VMEM, VMEM] if carried else []),
        out_specs=tuple(specs),
        scratch_shapes=[
            pltpu.VMEM((mp_count, count, width), BF16),
            pltpu.VMEM((count, width), BF16),
            pltpu.VMEM((count, width), BF16),
            pltpu.VMEM((count if not ring else BLOCK, mp_count * width), BF16),
            pltpu.VMEM((count, width), BF16),
            pltpu.VMEM((count, width), BF16),
            pltpu.VMEM((key_rows, width), BF16),
            pltpu.VMEM((key_rows, width), BF16),
            pltpu.SemaphoreType.DMA((blocks,)),
            pltpu.SemaphoreType.DMA(()),
            pltpu.SemaphoreType.DMA(()),
            pltpu.SemaphoreType.DMA((blocks,)),
        ]
        + last,
        input_output_aliases=aliases,
        compiler_params=pltpu.CompilerParams(vmem_limit_bytes=60 * 1024 * 1024),
        name="attend_last" if ring else "attend_first",
    )(owners, me, tokens, q_weight, cotangent, got, *carried)


def ring_targets(size, rows):
    half = rows // 2
    far = size // 2
    out = [(far, 0, half), (far, half, half)]
    for hop in range(far - 1, 0, -1):
        out += [(hop, 0, rows), (size - hop, 0, rows)]
    return out + [(0, 0, rows)]


def ring_sum(terms, size):
    def send(x, by):
        return lax.ppermute(x, "mp", [(i, (i + by) % size) for i in range(size)])

    def add(*xs):
        return sum(x.astype(F32) for x in xs)

    half = terms[0].shape[0]
    right, left = send(terms[0], 1), send(terms[1], -1)
    for hop in range(1, size // 2):
        own_right, own_left = terms[2 * hop], terms[2 * hop + 1]
        if hop == 1:
            right = jnp.concatenate([add(own_right[:half], right), own_right[half:].astype(F32)])
            left = jnp.concatenate([own_left[:half].astype(F32), add(own_left[half:], left)])
        else:
            right, left = add(own_right, right), add(own_left, left)
        right, left = send(right.astype(BF16), 1), send(left.astype(BF16), -1)
    return add(terms[-1], right, left).astype(BF16)


def body(
    tokens, q_weight, snippet_keys, snippet_values, out_cotangent, neighbour_ids, snippet_slot
):
    dp_count, mp_count = lax.axis_size("dp"), lax.axis_size("mp")
    seq_len = tokens.shape[0]
    snip_count = snippet_keys.shape[0]
    gathered = lax.all_gather(tokens, "mp", axis=0, tiled=False)
    request, owners = request_rows(neighbour_ids.T, snippet_slot, snip_count, dp_count)
    wanted = lax.all_to_all(request, "dp", split_axis=0, concat_axis=0, tiled=True)
    picked = pick_rows(wanted, snippet_keys, snippet_values)
    got = lax.all_to_all(picked, "dp", split_axis=0, concat_axis=0, tiled=True)
    me = lax.axis_index("mp").astype(jnp.int32).reshape(1)
    split = seq_len // 2
    shared = (owners, me, gathered, q_weight, out_cotangent, got)
    attended, terms, *sums = attend((0, split), *shared, (), None)
    input_grad_first = lax.psum_scatter(terms, "mp", scatter_dimension=1, tiled=True)
    ring = ring_targets(mp_count, seq_len - split)
    attended, uses, *targets = attend((split, seq_len), *shared, (attended, *sums), ring)
    input_grad_last = ring_sum(targets, mp_count)
    back = lax.all_to_all(uses, "dp", split_axis=0, concat_axis=0, tiled=True)
    key_grad, value_grad = sum_uses(wanted, back, snip_count)
    input_grad = jnp.concatenate([input_grad_first, input_grad_last], axis=0)
    return (attended, input_grad, key_grad, value_grad)


def solution(mesh):
    return jax.shard_map(
        body,
        mesh=mesh,
        in_specs=(
            P("dp", "mp"),
            P(None, "mp"),
            P("dp", None, "mp"),
            P("dp", None, "mp"),
            P("dp", "mp"),
            P("dp", None),
            P(),
        ),
        out_specs=(P("dp", "mp"), P("dp", "mp"), P("dp", None, "mp"), P("dp", None, "mp")),
        check_vma=False,
    )
```

```python
import math

import jax
import jax.numpy as jnp
from jax import lax
from jax.experimental import pallas as pl
from jax.experimental.pallas import tpu as pltpu
from jax.sharding import PartitionSpec as P

DH = 128
SPAN = 64
NEIGH = 2
TILE = 2 * SPAN
BLOCK = 2 * TILE
LANES = 128
F32 = jnp.float32
BF16 = jnp.bfloat16

VMEM = pl.BlockSpec(memory_space=pltpu.MemorySpace.VMEM)
SMEM = pl.BlockSpec(memory_space=pltpu.MemorySpace.SMEM)
HBM = pl.BlockSpec(memory_space=pltpu.MemorySpace.HBM)


def dot_nt(a, b):
    return lax.dot_general(a, b, (((1,), (1,)), ((), ())), preferred_element_type=F32)


def dot_tn(a, b):
    return lax.dot_general(a, b, (((0,), (0,)), ((), ())), preferred_element_type=F32)


def request_rows(ids, slot_table, snip_count, dp_count):
    spans = ids.shape[1]

    def kernel(ids_ref, slot_ref, req_ref, own_ref):
        def clear(i, c):
            req_ref[i, 0, 0] = 0
            return c

        lax.fori_loop(0, dp_count, clear, 0)

        def step(i, c):
            for n in range(NEIGH):
                slot = slot_ref[ids_ref[n, i]]
                owner = lax.div(slot, snip_count)
                req_ref[owner, 0, 0] = slot - owner * snip_count + 1
                own_ref[i * NEIGH + n] = owner
            return c

        lax.fori_loop(0, spans, step, 0)

    return pl.pallas_call(
        kernel,
        out_shape=(
            jax.ShapeDtypeStruct((dp_count, 1, LANES), jnp.int32),
            jax.ShapeDtypeStruct((spans * NEIGH,), jnp.int32),
        ),
        in_specs=[SMEM, SMEM],
        out_specs=(SMEM, SMEM),
        name="request_rows",
    )(ids, slot_table)


def pick_rows(wanted, keys, values):
    dp_count = wanted.shape[0]
    _, nei, width = keys.shape

    def kernel(want_ref, key_ref, value_ref, out_ref):
        def step(i, c):
            row = jnp.maximum(want_ref[i, 0, 0] - 1, 0)
            out_ref[i, :, :width] = key_ref[row]
            out_ref[i, :, width:] = value_ref[row]
            return c

        lax.fori_loop(0, dp_count, step, 0, unroll=4)

    return pl.pallas_call(
        kernel,
        out_shape=jax.ShapeDtypeStruct((dp_count, nei, 2 * width), keys.dtype),
        in_specs=[SMEM, VMEM, VMEM],
        out_specs=VMEM,
        name="pick_rows",
    )(wanted, keys, values)


def sum_uses(wanted, back, snip_count):
    dp_count, nei, twice = back.shape
    width = twice // 2

    def kernel(want_ref, back_ref, key_ref, value_ref):
        key_ref[...] = jnp.zeros_like(key_ref)
        value_ref[...] = jnp.zeros_like(value_ref)

        def step(i, c):
            want = want_ref[i, 0, 0]

            @pl.when(want > 0)
            def _():
                row = jnp.maximum(want - 1, 0)
                key_ref[row] += back_ref[i, :, :width].astype(F32)
                value_ref[row] += back_ref[i, :, width:].astype(F32)

            return c

        lax.fori_loop(0, dp_count, step, 0)

    out = jax.ShapeDtypeStruct((snip_count, nei, width), F32)
    return pl.pallas_call(
        kernel,
        out_shape=(out, out),
        in_specs=[SMEM, VMEM],
        out_specs=(VMEM, VMEM),
        name="sum_uses",
    )(wanted, back)


def tile_keys_of(t, span_keys):
    start = t * (TILE // SPAN) * span_keys
    return slice(start, start + (TILE // SPAN + 1) * span_keys)


def prepare(owners, cotangent, got):
    seq_len, width = cotangent.shape
    nei = got.shape[1]
    heads = width // DH
    picks = owners.shape[0]
    span_keys = NEIGH * nei
    tiles = seq_len // TILE
    padded = (seq_len // SPAN + 1) * span_keys
    tile_keys = (TILE // SPAN + 1) * span_keys

    def kernel(own_ref, cot_ref, got_ref, v_ref, k_ref, pg_ref):
        k_ref[:span_keys, :] = jnp.zeros((span_keys, width), BF16)
        v_ref[:span_keys, :] = jnp.zeros((span_keys, width), BF16)
        for n in range(picks):
            at = span_keys + n * nei
            k_ref[at : at + nei, :] = got_ref[own_ref[n], :, :width]
            v_ref[at : at + nei, :] = got_ref[own_ref[n], :, width:]
        for t in range(tiles):
            rows = slice(t * TILE, (t + 1) * TILE)
            for h in range(heads):
                cols = slice(h * DH, (h + 1) * DH)
                pg_ref[t * heads + h] = dot_nt(v_ref[tile_keys_of(t, span_keys), cols], cot_ref[rows, cols])

    return pl.pallas_call(
        kernel,
        out_shape=(
            jax.ShapeDtypeStruct((padded, width), BF16),
            jax.ShapeDtypeStruct((padded, width), BF16),
            jax.ShapeDtypeStruct((tiles * heads, tile_keys, TILE), F32),
        ),
        in_specs=[SMEM, VMEM, VMEM],
        out_specs=(VMEM, VMEM, VMEM),
        compiler_params=pltpu.CompilerParams(vmem_limit_bytes=16 * 1024 * 1024),
        name="prepare",
    )(owners, cotangent, got)


def attend(tokens, q_weight, keys, prob_grads, seq_len, span_keys):
    mp_count, _, width = tokens.shape
    heads = width // DH
    blocks = seq_len // BLOCK
    tile_keys = prob_grads.shape[1]
    scaling = 1.0 / math.sqrt(DH)

    def kernel(
        tok_hbm, w_ref, k_ref, pg_ref, term_hbm, q_hbm, pair_hbm,
        tok_ref, term_ref, q_ref, pair_ref, qg_ref, in_sem, out_sem, keep_sem,
    ):
        def load(b):
            rows = slice(b * BLOCK, (b + 1) * BLOCK)
            return pltpu.make_async_copy(tok_hbm.at[:, rows, :], tok_ref.at[:, rows, :], in_sem.at[b])

        def store(b):
            rows = slice(b * BLOCK, (b + 1) * BLOCK)
            return pltpu.make_async_copy(term_ref.at[rows, :], term_hbm.at[rows, :], out_sem.at[b])

        for b in range(blocks):
            load(b).start()
        key_at = lax.broadcasted_iota(jnp.int32, (tile_keys, TILE), 0) // span_keys
        span_of = (lax.broadcasted_iota(jnp.int32, (tile_keys, TILE), 1) + 1) // SPAN
        inner = key_at == span_of
        first_tile = inner & (key_at > 0)

        def one_tile(t):
            rows = slice(t * TILE, (t + 1) * TILE)
            for h in range(heads):
                cols = slice(h * DH, (h + 1) * DH)
                k = k_ref[tile_keys_of(t, span_keys), cols]
                scores = dot_nt(k, q_ref[rows, cols]) * scaling
                scores = jnp.where(inner if t else first_tile, scores, -jnp.inf)
                top = jnp.max(scores, axis=0, keepdims=True)
                if t == 0:
                    top = jnp.where(top == -jnp.inf, 0.0, top)
                grown = jnp.exp(scores - top)
                total = jnp.sum(grown, axis=0, keepdims=True)
                if t == 0:
                    total = jnp.where(total > 0.0, total, 1.0)
                weights = grown * (1.0 / total)
                prob_grad = pg_ref[t * heads + h]
                row_delta = jnp.sum(weights * prob_grad, axis=0, keepdims=True)
                score_grad = (weights * (prob_grad - row_delta)).astype(BF16)
                pair_ref[0, t * heads + h] = weights.astype(BF16)
                pair_ref[1, t * heads + h] = score_grad
                qg_ref[rows, cols] = (dot_tn(score_grad, k) * scaling).astype(BF16)

        for b in range(blocks):
            rows = slice(b * BLOCK, (b + 1) * BLOCK)
            load(b).wait()
            x = jnp.concatenate([tok_ref[j, rows, :] for j in range(mp_count)], axis=1)
            q_ref[rows, :] = jnp.dot(x, w_ref[...], preferred_element_type=F32).astype(BF16)
            for t in range(b * BLOCK // TILE, (b + 1) * BLOCK // TILE):
                one_tile(t)
            if b == blocks - 1:
                keep = [
                    pltpu.make_async_copy(q_ref, q_hbm, keep_sem.at[0]),
                    pltpu.make_async_copy(pair_ref, pair_hbm, keep_sem.at[1]),
                ]
                for copy in keep:
                    copy.start()
            term_ref[rows, :] = dot_nt(qg_ref[rows, :], w_ref[...]).astype(BF16)
            store(b).start()
        for b in range(blocks):
            store(b).wait()
        for copy in keep:
            copy.wait()

    return pl.pallas_call(
        kernel,
        out_shape=(
            pltpu.HBM((seq_len, mp_count * width), BF16),
            pltpu.HBM((seq_len, width), BF16),
            pltpu.HBM((2, *prob_grads.shape), BF16),
        ),
        in_specs=[HBM, VMEM, VMEM, VMEM],
        out_specs=(HBM, HBM, HBM),
        scratch_shapes=[
            pltpu.VMEM((mp_count, seq_len, width), BF16),
            pltpu.VMEM((seq_len, mp_count * width), BF16),
            pltpu.VMEM((seq_len, width), BF16),
            pltpu.VMEM((2, *prob_grads.shape), BF16),
            pltpu.VMEM((seq_len, width), BF16),
            pltpu.SemaphoreType.DMA((blocks,)),
            pltpu.SemaphoreType.DMA((blocks,)),
            pltpu.SemaphoreType.DMA((2,)),
        ],
        compiler_params=pltpu.CompilerParams(vmem_limit_bytes=24 * 1024 * 1024),
        name="attend",
    )(pltpu.with_memory_space_constraint(tokens, pltpu.HBM), q_weight, keys, prob_grads)


def finish(owners, queries, pairs, values, cotangent, dp_count):
    seq_len, width = cotangent.shape
    heads = width // DH
    tiles = seq_len // TILE
    picks = owners.shape[0]
    span_keys = values.shape[0] // (seq_len // SPAN + 1)
    nei = span_keys // NEIGH
    scaling = 1.0 / math.sqrt(DH)

    def kernel(own_ref, q_ref, pair_ref, v_ref, cot_ref, att_ref, use_ref, ku_ref, vu_ref):
        use_ref[...] = jnp.zeros_like(use_ref)
        for t in range(tiles):
            rows = slice(t * TILE, (t + 1) * TILE)
            keys_at = tile_keys_of(t, span_keys)
            start, mid, end = keys_at.start, keys_at.start + span_keys, keys_at.stop
            for h in range(heads):
                cols = slice(h * DH, (h + 1) * DH)
                p = pair_ref[0, t * heads + h]
                key_use = jnp.dot(pair_ref[1, t * heads + h], q_ref[rows, cols], preferred_element_type=F32)
                value_use = jnp.dot(p, cot_ref[rows, cols], preferred_element_type=F32)
                att_ref[rows, cols] = dot_tn(p, v_ref[keys_at, cols]).astype(BF16)
                if t == 0:
                    ku_ref[start:mid, cols] = key_use[:span_keys]
                    vu_ref[start:mid, cols] = value_use[:span_keys]
                else:
                    ku_ref[start:mid, cols] += key_use[:span_keys]
                    vu_ref[start:mid, cols] += value_use[:span_keys]
                ku_ref[mid:end, cols] = key_use[span_keys:]
                vu_ref[mid:end, cols] = value_use[span_keys:]
        for n in range(picks):
            at = span_keys + n * nei
            use_ref[own_ref[n], :, :width] = (ku_ref[at : at + nei, :] * scaling).astype(BF16)
            use_ref[own_ref[n], :, width:] = vu_ref[at : at + nei, :].astype(BF16)

    return pl.pallas_call(
        kernel,
        out_shape=(
            jax.ShapeDtypeStruct((seq_len, width), BF16),
            jax.ShapeDtypeStruct((dp_count, nei, 2 * width), BF16),
        ),
        in_specs=[SMEM] + [VMEM] * 4,
        out_specs=(VMEM, VMEM),
        scratch_shapes=[pltpu.VMEM(values.shape, F32), pltpu.VMEM(values.shape, F32)],
        compiler_params=pltpu.CompilerParams(vmem_limit_bytes=16 * 1024 * 1024),
        name="finish",
    )(owners, queries, pairs, values, cotangent)


def body(
    tokens, q_weight, snippet_keys, snippet_values, out_cotangent, neighbour_ids, snippet_slot
):
    dp_count = lax.axis_size("dp")
    seq_len = tokens.shape[0]
    snip_count, nei, _ = snippet_keys.shape
    gathered = lax.all_gather(tokens, "mp", axis=0, tiled=False)
    request, owners = request_rows(neighbour_ids.T, snippet_slot, snip_count, dp_count)
    wanted = lax.all_to_all(request, "dp", split_axis=0, concat_axis=0, tiled=True)
    picked = pick_rows(wanted, snippet_keys, snippet_values)
    got = lax.all_to_all(picked, "dp", split_axis=0, concat_axis=0, tiled=True)
    values, keys, prob_grads = prepare(owners, out_cotangent, got)
    terms, queries, pairs = attend(
        gathered, q_weight, keys, prob_grads, seq_len, NEIGH * nei
    )
    input_grad = lax.psum_scatter(terms, "mp", scatter_dimension=1, tiled=True)
    attended, uses = finish(
        owners, queries, pairs, values, out_cotangent, dp_count
    )
    back = lax.all_to_all(uses, "dp", split_axis=0, concat_axis=0, tiled=True)
    key_grad, value_grad = sum_uses(wanted, back, snip_count)
    return (attended, input_grad, key_grad, value_grad)


def solution(mesh):
    return jax.shard_map(
        body,
        mesh=mesh,
        in_specs=(
            P("dp", "mp"),
            P(None, "mp"),
            P("dp", None, "mp"),
            P("dp", None, "mp"),
            P("dp", "mp"),
            P("dp", None),
            P(),
        ),
        out_specs=(P("dp", "mp"), P("dp", "mp"), P("dp", None, "mp"), P("dp", None, "mp")),
        check_vma=False,
    )
```

```python
import math

import jax
import jax.numpy as jnp
from jax import lax
from jax.experimental import pallas as pl
from jax.experimental.pallas import tpu as pltpu
from jax.sharding import PartitionSpec as P

DH = 128
SPAN = 64
NEIGH = 2
TILE = 2 * SPAN
BLOCK = 2 * TILE
LANES = 128
F32 = jnp.float32
BF16 = jnp.bfloat16

VMEM = pl.BlockSpec(memory_space=pltpu.MemorySpace.VMEM)
SMEM = pl.BlockSpec(memory_space=pltpu.MemorySpace.SMEM)
HBM = pl.BlockSpec(memory_space=pltpu.MemorySpace.HBM)


def dot_nt(a, b):
    return lax.dot_general(a, b, (((1,), (1,)), ((), ())), preferred_element_type=F32)


def dot_tn(a, b):
    return lax.dot_general(a, b, (((0,), (0,)), ((), ())), preferred_element_type=F32)


def request_rows(ids, slot_table, snip_count, dp_count):
    spans = ids.shape[1]

    def kernel(ids_ref, slot_ref, req_ref, own_ref):
        def clear(i, c):
            req_ref[i, 0, 0] = 0
            return c

        lax.fori_loop(0, dp_count, clear, 0)

        def step(i, c):
            for n in range(NEIGH):
                slot = slot_ref[ids_ref[n, i]]
                owner = lax.div(slot, snip_count)
                req_ref[owner, 0, 0] = slot - owner * snip_count + 1
                own_ref[i * NEIGH + n] = owner
            return c

        lax.fori_loop(0, spans, step, 0)

    return pl.pallas_call(
        kernel,
        out_shape=(
            jax.ShapeDtypeStruct((dp_count, 1, LANES), jnp.int32),
            jax.ShapeDtypeStruct((spans * NEIGH,), jnp.int32),
        ),
        in_specs=[SMEM, SMEM],
        out_specs=(SMEM, SMEM),
        name="request_rows",
    )(ids, slot_table)


def pick_rows(wanted, keys, values):
    dp_count = wanted.shape[0]
    _, nei, width = keys.shape

    def kernel(want_ref, key_ref, value_ref, out_ref):
        def step(i, c):
            row = jnp.maximum(want_ref[i, 0, 0] - 1, 0)
            out_ref[i, :, :width] = key_ref[row]
            out_ref[i, :, width:] = value_ref[row]
            return c

        lax.fori_loop(0, dp_count, step, 0, unroll=4)

    return pl.pallas_call(
        kernel,
        out_shape=jax.ShapeDtypeStruct((dp_count, nei, 2 * width), keys.dtype),
        in_specs=[SMEM, VMEM, VMEM],
        out_specs=VMEM,
        name="pick_rows",
    )(wanted, keys, values)


def sum_uses(wanted, back, snip_count):
    dp_count, nei, twice = back.shape
    width = twice // 2

    def kernel(want_ref, back_ref, key_ref, value_ref):
        key_ref[...] = jnp.zeros_like(key_ref)
        value_ref[...] = jnp.zeros_like(value_ref)

        def step(i, c):
            want = want_ref[i, 0, 0]

            @pl.when(want > 0)
            def _():
                row = jnp.maximum(want - 1, 0)
                key_ref[row] += back_ref[i, :, :width].astype(F32)
                value_ref[row] += back_ref[i, :, width:].astype(F32)

            return c

        lax.fori_loop(0, dp_count, step, 0)

    out = jax.ShapeDtypeStruct((snip_count, nei, width), F32)
    return pl.pallas_call(
        kernel,
        out_shape=(out, out),
        in_specs=[SMEM, VMEM],
        out_specs=(VMEM, VMEM),
        name="sum_uses",
    )(wanted, back)


def tile_keys_of(t, span_keys):
    start = t * (TILE // SPAN) * span_keys
    return slice(start, start + (TILE // SPAN + 1) * span_keys)


def prepare(owners, cotangent, got):
    seq_len, width = cotangent.shape
    nei = got.shape[1]
    heads = width // DH
    picks = owners.shape[0]
    span_keys = NEIGH * nei
    tiles = seq_len // TILE
    padded = (seq_len // SPAN + 1) * span_keys
    tile_keys = (TILE // SPAN + 1) * span_keys

    def kernel(own_ref, cot_ref, got_ref, v_ref, k_ref, pg_ref):
        k_ref[:span_keys, :] = jnp.zeros((span_keys, width), BF16)
        v_ref[:span_keys, :] = jnp.zeros((span_keys, width), BF16)
        for n in range(picks):
            at = span_keys + n * nei
            k_ref[at : at + nei, :] = got_ref[own_ref[n], :, :width]
            v_ref[at : at + nei, :] = got_ref[own_ref[n], :, width:]
        for t in range(tiles):
            rows = slice(t * TILE, (t + 1) * TILE)
            for h in range(heads):
                cols = slice(h * DH, (h + 1) * DH)
                pg_ref[t * heads + h] = dot_nt(v_ref[tile_keys_of(t, span_keys), cols], cot_ref[rows, cols])

    return pl.pallas_call(
        kernel,
        out_shape=(
            jax.ShapeDtypeStruct((padded, width), BF16),
            jax.ShapeDtypeStruct((padded, width), BF16),
            jax.ShapeDtypeStruct((tiles * heads, tile_keys, TILE), F32),
        ),
        in_specs=[SMEM, VMEM, VMEM],
        out_specs=(VMEM, VMEM, VMEM),
        compiler_params=pltpu.CompilerParams(vmem_limit_bytes=16 * 1024 * 1024),
        name="prepare",
    )(owners, cotangent, got)


def attend(tokens, q_weight, keys, prob_grads, seq_len, span_keys):
    mp_count, _, width = tokens.shape
    heads = width // DH
    blocks = seq_len // BLOCK
    tile_keys = prob_grads.shape[1]
    scaling = 1.0 / math.sqrt(DH)

    def kernel(
        tok_hbm, w_ref, k_ref, pg_ref, term_hbm, q_hbm, pair_hbm,
        tok_ref, term_ref, q_ref, pair_ref, qg_ref, s_ref, in_sem, out_sem, keep_sem,
    ):
        def load(b):
            rows = slice(b * BLOCK, (b + 1) * BLOCK)
            return pltpu.make_async_copy(tok_hbm.at[:, rows, :], tok_ref.at[:, rows, :], in_sem.at[b])

        def store(b):
            rows = slice(b * BLOCK, (b + 1) * BLOCK)
            return pltpu.make_async_copy(term_ref.at[rows, :], term_hbm.at[rows, :], out_sem.at[b])

        for b in range(blocks):
            load(b).start()
        key_at = lax.broadcasted_iota(jnp.int32, (tile_keys, TILE), 0) // span_keys
        span_of = (lax.broadcasted_iota(jnp.int32, (tile_keys, TILE), 1) + 1) // SPAN
        inner = key_at == span_of
        first_tile = inner & (key_at > 0)

        def places(b):
            for t in range(b * BLOCK // TILE, (b + 1) * BLOCK // TILE):
                for h in range(heads):
                    yield t, t * heads + h, slice(t * TILE, (t + 1) * TILE), slice(h * DH, (h + 1) * DH)

        def score(b):
            for t, i, rows, cols in places(b):
                s_ref[i] = dot_nt(k_ref[tile_keys_of(t, span_keys), cols], q_ref[rows, cols])

        def weigh(b):
            for t, i, rows, cols in places(b):
                scores = jnp.where(inner if t else first_tile, s_ref[i] * scaling, -jnp.inf)
                top = jnp.max(scores, axis=0, keepdims=True)
                if t == 0:
                    top = jnp.where(top == -jnp.inf, 0.0, top)
                grown = jnp.exp(scores - top)
                total = jnp.sum(grown, axis=0, keepdims=True)
                if t == 0:
                    total = jnp.where(total > 0.0, total, 1.0)
                weights = grown * (1.0 / total)
                prob_grad = pg_ref[i]
                row_delta = jnp.sum(weights * prob_grad, axis=0, keepdims=True)
                pair_ref[0, i] = weights.astype(BF16)
                pair_ref[1, i] = (weights * (prob_grad - row_delta)).astype(BF16)

        def grad(b):
            for t, i, rows, cols in places(b):
                k = k_ref[tile_keys_of(t, span_keys), cols]
                qg_ref[rows, cols] = (dot_tn(pair_ref[1, i], k) * scaling).astype(BF16)

        def project(b):
            rows = slice(b * BLOCK, (b + 1) * BLOCK)
            load(b).wait()
            x = jnp.concatenate([tok_ref[j, rows, :] for j in range(mp_count)], axis=1)
            q_ref[rows, :] = jnp.dot(x, w_ref[...], preferred_element_type=F32).astype(BF16)

        def spread(b):
            rows = slice(b * BLOCK, (b + 1) * BLOCK)
            term_ref[rows, :] = dot_nt(qg_ref[rows, :], w_ref[...]).astype(BF16)
            store(b).start()

        keep = [
            pltpu.make_async_copy(q_ref, q_hbm, keep_sem.at[0]),
            pltpu.make_async_copy(pair_ref, pair_hbm, keep_sem.at[1]),
        ]
        project(0)
        project(1)
        project(2)
        project(3)
        score(0)
        score(1)
        score(2)
        score(3)
        weigh(0)
        weigh(1)
        grad(0)
        grad(1)
        spread(0)
        spread(1)
        weigh(2)
        weigh(3)
        grad(2)
        grad(3)
        for copy in keep:
            copy.start()
        spread(2)
        spread(3)
        for b in range(blocks):
            store(b).wait()
        for copy in keep:
            copy.wait()

    return pl.pallas_call(
        kernel,
        out_shape=(
            pltpu.HBM((seq_len, mp_count * width), BF16),
            pltpu.HBM((seq_len, width), BF16),
            pltpu.HBM((2, *prob_grads.shape), BF16),
        ),
        in_specs=[HBM, VMEM, VMEM, VMEM],
        out_specs=(HBM, HBM, HBM),
        scratch_shapes=[
            pltpu.VMEM((mp_count, seq_len, width), BF16),
            pltpu.VMEM((seq_len, mp_count * width), BF16),
            pltpu.VMEM((seq_len, width), BF16),
            pltpu.VMEM((2, *prob_grads.shape), BF16),
            pltpu.VMEM((seq_len, width), BF16),
            pltpu.VMEM(prob_grads.shape, F32),
            pltpu.SemaphoreType.DMA((blocks,)),
            pltpu.SemaphoreType.DMA((blocks,)),
            pltpu.SemaphoreType.DMA((2,)),
        ],
        compiler_params=pltpu.CompilerParams(vmem_limit_bytes=24 * 1024 * 1024),
        name="attend",
    )(pltpu.with_memory_space_constraint(tokens, pltpu.HBM), q_weight, keys, prob_grads)


def finish(owners, queries, pairs, values, cotangent, dp_count):
    seq_len, width = cotangent.shape
    heads = width // DH
    tiles = seq_len // TILE
    picks = owners.shape[0]
    span_keys = values.shape[0] // (seq_len // SPAN + 1)
    nei = span_keys // NEIGH
    scaling = 1.0 / math.sqrt(DH)

    def kernel(own_ref, q_ref, pair_ref, v_ref, cot_ref, att_ref, use_ref, ku_ref, vu_ref):
        use_ref[...] = jnp.zeros_like(use_ref)
        for t in range(tiles):
            rows = slice(t * TILE, (t + 1) * TILE)
            keys_at = tile_keys_of(t, span_keys)
            start, mid, end = keys_at.start, keys_at.start + span_keys, keys_at.stop
            for h in range(heads):
                cols = slice(h * DH, (h + 1) * DH)
                p = pair_ref[0, t * heads + h]
                key_use = jnp.dot(pair_ref[1, t * heads + h], q_ref[rows, cols], preferred_element_type=F32)
                value_use = jnp.dot(p, cot_ref[rows, cols], preferred_element_type=F32)
                att_ref[rows, cols] = dot_tn(p, v_ref[keys_at, cols]).astype(BF16)
                if t == 0:
                    ku_ref[start:mid, cols] = key_use[:span_keys]
                    vu_ref[start:mid, cols] = value_use[:span_keys]
                else:
                    ku_ref[start:mid, cols] += key_use[:span_keys]
                    vu_ref[start:mid, cols] += value_use[:span_keys]
                ku_ref[mid:end, cols] = key_use[span_keys:]
                vu_ref[mid:end, cols] = value_use[span_keys:]
        for n in range(picks):
            at = span_keys + n * nei
            use_ref[own_ref[n], :, :width] = (ku_ref[at : at + nei, :] * scaling).astype(BF16)
            use_ref[own_ref[n], :, width:] = vu_ref[at : at + nei, :].astype(BF16)

    return pl.pallas_call(
        kernel,
        out_shape=(
            jax.ShapeDtypeStruct((seq_len, width), BF16),
            jax.ShapeDtypeStruct((dp_count, nei, 2 * width), BF16),
        ),
        in_specs=[SMEM] + [VMEM] * 4,
        out_specs=(VMEM, VMEM),
        scratch_shapes=[pltpu.VMEM(values.shape, F32), pltpu.VMEM(values.shape, F32)],
        compiler_params=pltpu.CompilerParams(vmem_limit_bytes=16 * 1024 * 1024),
        name="finish",
    )(owners, queries, pairs, values, cotangent)


def body(
    tokens, q_weight, snippet_keys, snippet_values, out_cotangent, neighbour_ids, snippet_slot
):
    dp_count = lax.axis_size("dp")
    seq_len = tokens.shape[0]
    snip_count, nei, _ = snippet_keys.shape
    gathered = lax.all_gather(tokens, "mp", axis=0, tiled=False)
    request, owners = request_rows(neighbour_ids.T, snippet_slot, snip_count, dp_count)
    wanted = lax.all_to_all(request, "dp", split_axis=0, concat_axis=0, tiled=True)
    picked = pick_rows(wanted, snippet_keys, snippet_values)
    got = lax.all_to_all(picked, "dp", split_axis=0, concat_axis=0, tiled=True)
    values, keys, prob_grads = prepare(owners, out_cotangent, got)
    terms, queries, pairs = attend(
        gathered, q_weight, keys, prob_grads, seq_len, NEIGH * nei
    )
    input_grad = lax.psum_scatter(terms, "mp", scatter_dimension=1, tiled=True)
    attended, uses = finish(
        owners, queries, pairs, values, out_cotangent, dp_count
    )
    back = lax.all_to_all(uses, "dp", split_axis=0, concat_axis=0, tiled=True)
    key_grad, value_grad = sum_uses(wanted, back, snip_count)
    return (attended, input_grad, key_grad, value_grad)


def solution(mesh):
    return jax.shard_map(
        body,
        mesh=mesh,
        in_specs=(
            P("dp", "mp"),
            P(None, "mp"),
            P("dp", None, "mp"),
            P("dp", None, "mp"),
            P("dp", "mp"),
            P("dp", None),
            P(),
        ),
        out_specs=(P("dp", "mp"), P("dp", "mp"), P("dp", None, "mp"), P("dp", None, "mp")),
        check_vma=False,
    )
```

```python
import math

import jax
import jax.numpy as jnp
from jax import lax
from jax.experimental import pallas as pl
from jax.experimental.pallas import tpu as pltpu
from jax.sharding import PartitionSpec as P

DH = 128
SPAN = 64
NEIGH = 2
TILE = 2 * SPAN
BLOCK = 2 * TILE
LANES = 128
F32 = jnp.float32
BF16 = jnp.bfloat16

VMEM = pl.BlockSpec(memory_space=pltpu.MemorySpace.VMEM)
SMEM = pl.BlockSpec(memory_space=pltpu.MemorySpace.SMEM)
HBM = pl.BlockSpec(memory_space=pltpu.MemorySpace.HBM)


def dot_nt(a, b):
    return lax.dot_general(a, b, (((1,), (1,)), ((), ())), preferred_element_type=F32)


def dot_tn(a, b):
    return lax.dot_general(a, b, (((0,), (0,)), ((), ())), preferred_element_type=F32)


def request_rows(ids, slot_table, snip_count, dp_count):
    spans = ids.shape[1]

    def kernel(ids_ref, slot_ref, req_ref, own_ref):
        def clear(i, c):
            req_ref[i, 0, 0] = 0
            return c

        lax.fori_loop(0, dp_count, clear, 0)

        def step(i, c):
            for n in range(NEIGH):
                slot = slot_ref[ids_ref[n, i]]
                owner = lax.div(slot, snip_count)
                req_ref[owner, 0, 0] = slot - owner * snip_count + 1
                own_ref[i * NEIGH + n] = owner
            return c

        lax.fori_loop(0, spans, step, 0)

    return pl.pallas_call(
        kernel,
        out_shape=(
            jax.ShapeDtypeStruct((dp_count, 1, LANES), jnp.int32),
            jax.ShapeDtypeStruct((spans * NEIGH,), jnp.int32),
        ),
        in_specs=[SMEM, SMEM],
        out_specs=(SMEM, SMEM),
        name="request_rows",
    )(ids, slot_table)


def pick_rows(wanted, keys, values):
    dp_count = wanted.shape[0]
    _, nei, width = keys.shape

    def kernel(want_ref, key_ref, value_ref, out_ref):
        def step(i, c):
            row = jnp.maximum(want_ref[i, 0, 0] - 1, 0)
            out_ref[i, :, :width] = key_ref[row]
            out_ref[i, :, width:] = value_ref[row]
            return c

        lax.fori_loop(0, dp_count, step, 0, unroll=4)

    return pl.pallas_call(
        kernel,
        out_shape=jax.ShapeDtypeStruct((dp_count, nei, 2 * width), keys.dtype),
        in_specs=[SMEM, VMEM, VMEM],
        out_specs=VMEM,
        name="pick_rows",
    )(wanted, keys, values)


def sum_uses(wanted, back, snip_count):
    dp_count, nei, twice = back.shape
    width = twice // 2

    def kernel(want_ref, back_ref, key_ref, value_ref):
        key_ref[...] = jnp.zeros_like(key_ref)
        value_ref[...] = jnp.zeros_like(value_ref)

        def step(i, c):
            want = want_ref[i, 0, 0]

            @pl.when(want > 0)
            def _():
                row = jnp.maximum(want - 1, 0)
                key_ref[row] += back_ref[i, :, :width].astype(F32)
                value_ref[row] += back_ref[i, :, width:].astype(F32)

            return c

        lax.fori_loop(0, dp_count, step, 0)

    out = jax.ShapeDtypeStruct((snip_count, nei, width), F32)
    return pl.pallas_call(
        kernel,
        out_shape=(out, out),
        in_specs=[SMEM, VMEM],
        out_specs=(VMEM, VMEM),
        name="sum_uses",
    )(wanted, back)


def tile_keys_of(t, span_keys):
    start = t * (TILE // SPAN) * span_keys
    return slice(start, start + (TILE // SPAN + 1) * span_keys)


def prepare(owners, cotangent, got):
    seq_len, width = cotangent.shape
    nei = got.shape[1]
    heads = width // DH
    picks = owners.shape[0]
    span_keys = NEIGH * nei
    tiles = seq_len // TILE
    padded = (seq_len // SPAN + 1) * span_keys
    tile_keys = (TILE // SPAN + 1) * span_keys

    def kernel(own_ref, cot_ref, got_ref, v_ref, k_ref, pg_ref):
        k_ref[:span_keys, :] = jnp.zeros((span_keys, width), BF16)
        v_ref[:span_keys, :] = jnp.zeros((span_keys, width), BF16)
        for n in range(picks):
            at = span_keys + n * nei
            k_ref[at : at + nei, :] = got_ref[own_ref[n], :, :width]
            v_ref[at : at + nei, :] = got_ref[own_ref[n], :, width:]
        for t in range(tiles):
            rows = slice(t * TILE, (t + 1) * TILE)
            for h in range(heads):
                cols = slice(h * DH, (h + 1) * DH)
                pg_ref[t * heads + h] = dot_nt(v_ref[tile_keys_of(t, span_keys), cols], cot_ref[rows, cols])

    return pl.pallas_call(
        kernel,
        out_shape=(
            jax.ShapeDtypeStruct((padded, width), BF16),
            jax.ShapeDtypeStruct((padded, width), BF16),
            jax.ShapeDtypeStruct((tiles * heads, tile_keys, TILE), F32),
        ),
        in_specs=[SMEM, VMEM, VMEM],
        out_specs=(VMEM, VMEM, VMEM),
        compiler_params=pltpu.CompilerParams(vmem_limit_bytes=16 * 1024 * 1024),
        name="prepare",
    )(owners, cotangent, got)


def tile_places(seq_len, heads, low, high):
    for t in range(low // TILE, high // TILE):
        for h in range(heads):
            yield t, t * heads + h, slice(t * TILE, (t + 1) * TILE), slice(h * DH, (h + 1) * DH)


def attends(tile_keys, span_keys):
    key_at = lax.broadcasted_iota(jnp.int32, (tile_keys, TILE), 0) // span_keys
    span_of = (lax.broadcasted_iota(jnp.int32, (tile_keys, TILE), 1) + 1) // SPAN
    inner = key_at == span_of
    return inner, inner & (key_at > 0)


def weigh(products, prob_grad, masks, t):
    scores = jnp.where(masks[0] if t else masks[1], products * (1.0 / math.sqrt(DH)), -jnp.inf)
    top = jnp.max(scores, axis=0, keepdims=True)
    if t == 0:
        top = jnp.where(top == -jnp.inf, 0.0, top)
    grown = jnp.exp(scores - top)
    total = jnp.sum(grown, axis=0, keepdims=True)
    if t == 0:
        total = jnp.where(total > 0.0, total, 1.0)
    weights = grown * (1.0 / total)
    row_delta = jnp.sum(weights * prob_grad, axis=0, keepdims=True)
    return weights.astype(BF16), (weights * (prob_grad - row_delta)).astype(BF16)


def attend(tokens, q_weight, keys, prob_grads, seq_len, span_keys):
    mp_count, given, width = tokens.shape
    heads = width // DH
    blocks = seq_len // BLOCK
    tile_keys = prob_grads.shape[1]
    scaling = 1.0 / math.sqrt(DH)
    skip = seq_len - given
    half = seq_len // 2

    def kernel(
        tok_hbm, w_ref, k_ref, pg_ref, term_hbm, q_hbm,
        tok_ref, term_ref, q_ref, sg_ref, qg_ref, s_ref, in_sem, out_sem, keep_sem,
    ):
        def load(i):
            low, high = (half, seq_len) if i else (skip, half)
            source = tok_hbm.at[:, low - skip : high - skip, :]
            return pltpu.make_async_copy(source, tok_ref.at[:, low:high, :], in_sem.at[i])

        def store(b):
            rows = slice(b * BLOCK, (b + 1) * BLOCK)
            return pltpu.make_async_copy(term_ref.at[rows, :], term_hbm.at[rows, :], out_sem.at[b])

        load(0).start()
        load(1).start()
        keep = pltpu.make_async_copy(q_ref, q_hbm, keep_sem)
        masks = attends(tile_keys, span_keys)
        if skip:
            q_ref[:skip, :] = jnp.zeros((skip, width), BF16)
        load(0).wait()
        for b in range(blocks):
            if b * BLOCK == half:
                load(1).wait()
            rows = slice(max(b * BLOCK, skip), (b + 1) * BLOCK)
            x = jnp.concatenate([tok_ref[j, rows, :] for j in range(mp_count)], axis=1)
            q_ref[rows, :] = jnp.dot(x, w_ref[...], preferred_element_type=F32).astype(BF16)
        keep.start()
        for t, i, rows, cols in tile_places(seq_len, heads, 0, seq_len):
            s_ref[i] = dot_nt(k_ref[tile_keys_of(t, span_keys), cols], q_ref[rows, cols])
        for low in (0, half):
            for t, i, rows, cols in tile_places(seq_len, heads, low, low + half):
                _, sg_ref[i] = weigh(s_ref[i], pg_ref[i], masks, t)
            for t, i, rows, cols in tile_places(seq_len, heads, low, low + half):
                k = k_ref[tile_keys_of(t, span_keys), cols]
                qg_ref[rows, cols] = (dot_tn(sg_ref[i], k) * scaling).astype(BF16)
            for b in range(low // BLOCK, (low + half) // BLOCK):
                rows = slice(b * BLOCK, (b + 1) * BLOCK)
                term_ref[rows, :] = dot_nt(qg_ref[rows, :], w_ref[...]).astype(BF16)
                store(b).start()
        for b in range(blocks):
            store(b).wait()
        keep.wait()

    return pl.pallas_call(
        kernel,
        out_shape=(
            pltpu.HBM((seq_len, mp_count * width), BF16),
            pltpu.HBM((seq_len, width), BF16),
        ),
        in_specs=[HBM, VMEM, VMEM, VMEM],
        out_specs=(HBM, HBM),
        scratch_shapes=[
            pltpu.VMEM((mp_count, seq_len, width), BF16),
            pltpu.VMEM((seq_len, mp_count * width), BF16),
            pltpu.VMEM((seq_len, width), BF16),
            pltpu.VMEM(prob_grads.shape, BF16),
            pltpu.VMEM((seq_len, width), BF16),
            pltpu.VMEM(prob_grads.shape, F32),
            pltpu.SemaphoreType.DMA((2,)),
            pltpu.SemaphoreType.DMA((blocks,)),
            pltpu.SemaphoreType.DMA(()),
        ],
        compiler_params=pltpu.CompilerParams(vmem_limit_bytes=24 * 1024 * 1024),
        name="attend",
    )(pltpu.with_memory_space_constraint(tokens, pltpu.HBM), q_weight, keys, prob_grads)


def finish(owners, queries, keys, values, prob_grads, cotangent, dp_count):
    seq_len, width = cotangent.shape
    heads = width // DH
    picks = owners.shape[0]
    span_keys = values.shape[0] // (seq_len // SPAN + 1)
    nei = span_keys // NEIGH
    tile_keys = prob_grads.shape[1]
    scaling = 1.0 / math.sqrt(DH)

    def kernel(
        own_ref, q_ref, k_ref, v_ref, pg_ref, cot_ref, att_ref, use_ref,
        s_ref, p_ref, sg_ref, ku_ref, vu_ref,
    ):
        use_ref[...] = jnp.zeros_like(use_ref)
        masks = attends(tile_keys, span_keys)
        for t, i, rows, cols in tile_places(seq_len, heads, 0, seq_len):
            s_ref[i] = dot_nt(k_ref[tile_keys_of(t, span_keys), cols], q_ref[rows, cols])
        for t, i, rows, cols in tile_places(seq_len, heads, 0, seq_len):
            p_ref[i], sg_ref[i] = weigh(s_ref[i], pg_ref[i], masks, t)
        for t, i, rows, cols in tile_places(seq_len, heads, 0, seq_len):
            keys_at = tile_keys_of(t, span_keys)
            start, mid, end = keys_at.start, keys_at.start + span_keys, keys_at.stop
            key_use = jnp.dot(sg_ref[i], q_ref[rows, cols], preferred_element_type=F32)
            value_use = jnp.dot(p_ref[i], cot_ref[rows, cols], preferred_element_type=F32)
            att_ref[rows, cols] = dot_tn(p_ref[i], v_ref[keys_at, cols]).astype(BF16)
            if t == 0:
                ku_ref[start:mid, cols] = key_use[:span_keys]
                vu_ref[start:mid, cols] = value_use[:span_keys]
            else:
                ku_ref[start:mid, cols] += key_use[:span_keys]
                vu_ref[start:mid, cols] += value_use[:span_keys]
            ku_ref[mid:end, cols] = key_use[span_keys:]
            vu_ref[mid:end, cols] = value_use[span_keys:]
        for n in range(picks):
            at = span_keys + n * nei
            use_ref[own_ref[n], :, :width] = (ku_ref[at : at + nei, :] * scaling).astype(BF16)
            use_ref[own_ref[n], :, width:] = vu_ref[at : at + nei, :].astype(BF16)

    return pl.pallas_call(
        kernel,
        out_shape=(
            jax.ShapeDtypeStruct((seq_len, width), BF16),
            jax.ShapeDtypeStruct((dp_count, nei, 2 * width), BF16),
        ),
        in_specs=[SMEM] + [VMEM] * 5,
        out_specs=(VMEM, VMEM),
        scratch_shapes=[
            pltpu.VMEM(prob_grads.shape, F32),
            pltpu.VMEM(prob_grads.shape, BF16),
            pltpu.VMEM(prob_grads.shape, BF16),
            pltpu.VMEM(values.shape, F32),
            pltpu.VMEM(values.shape, F32),
        ],
        compiler_params=pltpu.CompilerParams(vmem_limit_bytes=20 * 1024 * 1024),
        name="finish",
    )(owners, queries, keys, values, prob_grads, cotangent)


def body(
    tokens, q_weight, snippet_keys, snippet_values, out_cotangent, neighbour_ids, snippet_slot
):
    dp_count = lax.axis_size("dp")
    seq_len = tokens.shape[0]
    snip_count, nei, _ = snippet_keys.shape
    skip = (SPAN - 1) // 16 * 16
    gathered = lax.all_gather(tokens[skip:], "mp", axis=0, tiled=False)
    request, owners = request_rows(neighbour_ids.T, snippet_slot, snip_count, dp_count)
    wanted = lax.all_to_all(request, "dp", split_axis=0, concat_axis=0, tiled=True)
    picked = pick_rows(wanted, snippet_keys, snippet_values)
    got = lax.all_to_all(picked, "dp", split_axis=0, concat_axis=0, tiled=True)
    values, keys, prob_grads = prepare(owners, out_cotangent, got)
    terms, queries = attend(
        gathered, q_weight, keys, prob_grads, seq_len, NEIGH * nei
    )
    input_grad = lax.psum_scatter(terms, "mp", scatter_dimension=1, tiled=True)
    attended, uses = finish(
        owners, queries, keys, values, prob_grads, out_cotangent, dp_count
    )
    back = lax.all_to_all(uses, "dp", split_axis=0, concat_axis=0, tiled=True)
    key_grad, value_grad = sum_uses(wanted, back, snip_count)
    return (attended, input_grad, key_grad, value_grad)


def solution(mesh):
    return jax.shard_map(
        body,
        mesh=mesh,
        in_specs=(
            P("dp", "mp"),
            P(None, "mp"),
            P("dp", None, "mp"),
            P("dp", None, "mp"),
            P("dp", "mp"),
            P("dp", None),
            P(),
        ),
        out_specs=(P("dp", "mp"), P("dp", "mp"), P("dp", None, "mp"), P("dp", None, "mp")),
        check_vma=False,
    )
```

```python
import math

import jax
import jax.numpy as jnp
from jax import lax
from jax.experimental import pallas as pl
from jax.experimental.pallas import tpu as pltpu
from jax.sharding import PartitionSpec as P

DH = 128
SPAN = 64
NEIGH = 2
TILE = 2 * SPAN
BLOCK = 2 * TILE
LANES = 128
F32 = jnp.float32
BF16 = jnp.bfloat16

VMEM = pl.BlockSpec(memory_space=pltpu.MemorySpace.VMEM)
SMEM = pl.BlockSpec(memory_space=pltpu.MemorySpace.SMEM)
HBM = pl.BlockSpec(memory_space=pltpu.MemorySpace.HBM)


def dot_nt(a, b):
    return lax.dot_general(a, b, (((1,), (1,)), ((), ())), preferred_element_type=F32)


def dot_tn(a, b):
    return lax.dot_general(a, b, (((0,), (0,)), ((), ())), preferred_element_type=F32)


def request_rows(ids, slot_table, snip_count, dp_count):
    spans = ids.shape[1]

    def kernel(ids_ref, slot_ref, req_ref, own_ref):
        def clear(i, c):
            req_ref[i, 0, 0] = 0
            return c

        lax.fori_loop(0, dp_count, clear, 0, unroll=16)

        def step(i, c):
            for n in range(NEIGH):
                slot = slot_ref[ids_ref[n, i]]
                owner = lax.div(slot, snip_count)
                req_ref[owner, 0, 0] = slot - owner * snip_count + 1
                own_ref[i * NEIGH + n] = owner
            return c

        lax.fori_loop(0, spans, step, 0, unroll=4)

    return pl.pallas_call(
        kernel,
        out_shape=(
            jax.ShapeDtypeStruct((dp_count, 1, LANES), jnp.int32),
            jax.ShapeDtypeStruct((spans * NEIGH,), jnp.int32),
        ),
        in_specs=[SMEM, SMEM],
        out_specs=(SMEM, SMEM),
        name="request_rows",
    )(ids, slot_table)


def pick_rows(wanted, keys, values):
    dp_count = wanted.shape[0]
    _, nei, width = keys.shape

    def kernel(want_ref, key_ref, value_ref, out_ref):
        def step(i, c):
            row = jnp.maximum(want_ref[i, 0, 0] - 1, 0)
            out_ref[i, :, :width] = key_ref[row]
            out_ref[i, :, width:] = value_ref[row]
            return c

        lax.fori_loop(0, dp_count, step, 0, unroll=4)

    return pl.pallas_call(
        kernel,
        out_shape=pltpu.VMEM((dp_count, nei, 2 * width), keys.dtype),
        in_specs=[SMEM, VMEM, VMEM],
        out_specs=VMEM,
        name="pick_rows",
    )(wanted, keys, values)


def sum_uses(wanted, back, snip_count):
    dp_count, nei, twice = back.shape
    width = twice // 2

    def kernel(want_ref, back_ref, key_ref, value_ref):
        key_ref[...] = jnp.zeros_like(key_ref)
        value_ref[...] = jnp.zeros_like(value_ref)

        def step(i, c):
            want = want_ref[i, 0, 0]

            @pl.when(want > 0)
            def _():
                row = jnp.maximum(want - 1, 0)
                key_ref[row] += back_ref[i, :, :width].astype(F32)
                value_ref[row] += back_ref[i, :, width:].astype(F32)

            return c

        lax.fori_loop(0, dp_count, step, 0)

    out = jax.ShapeDtypeStruct((snip_count, nei, width), F32)
    return pl.pallas_call(
        kernel,
        out_shape=(out, out),
        in_specs=[SMEM, VMEM],
        out_specs=(VMEM, VMEM),
        name="sum_uses",
    )(wanted, back)


def tile_keys_of(t, span_keys):
    start = t * (TILE // SPAN) * span_keys
    return slice(start, start + (TILE // SPAN + 1) * span_keys)


def prepare(owners, cotangent, got):
    seq_len, width = cotangent.shape
    nei = got.shape[1]
    heads = width // DH
    picks = owners.shape[0]
    span_keys = NEIGH * nei
    tiles = seq_len // TILE
    padded = (seq_len // SPAN + 1) * span_keys
    tile_keys = (TILE // SPAN + 1) * span_keys

    def kernel(own_ref, cot_ref, got_ref, v_ref, k_ref, pg_ref):
        k_ref[:span_keys, :] = jnp.zeros((span_keys, width), BF16)
        v_ref[:span_keys, :] = jnp.zeros((span_keys, width), BF16)
        for n in range(picks):
            at = span_keys + n * nei
            k_ref[at : at + nei, :] = got_ref[own_ref[n], :, :width]
            v_ref[at : at + nei, :] = got_ref[own_ref[n], :, width:]
        for t in range(tiles):
            rows = slice(t * TILE, (t + 1) * TILE)
            for h in range(heads):
                cols = slice(h * DH, (h + 1) * DH)
                pg_ref[t * heads + h] = dot_nt(v_ref[tile_keys_of(t, span_keys), cols], cot_ref[rows, cols])

    return pl.pallas_call(
        kernel,
        out_shape=(
            jax.ShapeDtypeStruct((padded, width), BF16),
            jax.ShapeDtypeStruct((padded, width), BF16),
            jax.ShapeDtypeStruct((tiles * heads, tile_keys, TILE), F32),
        ),
        in_specs=[SMEM, VMEM, VMEM],
        out_specs=(VMEM, VMEM, VMEM),
        compiler_params=pltpu.CompilerParams(vmem_limit_bytes=16 * 1024 * 1024),
        name="prepare",
    )(pltpu.with_memory_space_constraint(owners, pltpu.HBM), cotangent, got)


def tile_places(seq_len, heads, low, high):
    for t in range(low // TILE, high // TILE):
        for h in range(heads):
            yield t, t * heads + h, slice(t * TILE, (t + 1) * TILE), slice(h * DH, (h + 1) * DH)


def attends(tile_keys, span_keys):
    key_at = lax.broadcasted_iota(jnp.int32, (tile_keys, TILE), 0) // span_keys
    span_of = (lax.broadcasted_iota(jnp.int32, (tile_keys, TILE), 1) + 1) // SPAN
    inner = key_at == span_of
    return inner, inner & (key_at > 0)


def weigh(products, prob_grad, masks, t):
    scores = jnp.where(masks[0] if t else masks[1], products * (1.0 / math.sqrt(DH)), -jnp.inf)
    top = jnp.max(scores, axis=0, keepdims=True)
    if t == 0:
        top = jnp.where(top == -jnp.inf, 0.0, top)
    grown = jnp.exp(scores - top)
    total = jnp.sum(grown, axis=0, keepdims=True)
    if t == 0:
        total = jnp.where(total > 0.0, total, 1.0)
    weights = grown * (1.0 / total)
    row_delta = jnp.sum(weights * prob_grad, axis=0, keepdims=True)
    return weights.astype(BF16), (weights * (prob_grad - row_delta)).astype(BF16)


def attend(tokens, q_weight, keys, prob_grads, seq_len, span_keys):
    mp_count, _, width = tokens.shape
    heads = width // DH
    blocks = seq_len // BLOCK
    tile_keys = prob_grads.shape[1]
    scaling = 1.0 / math.sqrt(DH)
    skip = (SPAN - 1) // 16 * 16
    half = seq_len // 2

    def kernel(
        tok_hbm, w_ref, k_ref, pg_ref, term_hbm, q_hbm,
        tok_ref, term_ref, q_ref, sg_ref, qg_ref, s_ref, in_sem, out_sem, keep_sem,
    ):
        def load(i):
            low, high = (half, seq_len) if i else (skip, half)
            source = tok_hbm.at[:, low:high, :]
            return pltpu.make_async_copy(source, tok_ref.at[:, low:high, :], in_sem.at[i])

        def store(b):
            rows = slice(b * BLOCK, (b + 1) * BLOCK)
            return pltpu.make_async_copy(term_ref.at[rows, :], term_hbm.at[rows, :], out_sem.at[b])

        load(0).start()
        load(1).start()
        keep = pltpu.make_async_copy(q_ref, q_hbm, keep_sem)
        masks = attends(tile_keys, span_keys)
        q_ref[:skip, :] = jnp.zeros((skip, width), BF16)
        load(0).wait()
        for b in range(blocks):
            if b * BLOCK == half:
                load(1).wait()
            rows = slice(max(b * BLOCK, skip), (b + 1) * BLOCK)
            x = jnp.concatenate([tok_ref[j, rows, :] for j in range(mp_count)], axis=1)
            q_ref[rows, :] = jnp.dot(x, w_ref[...], preferred_element_type=F32).astype(BF16)
        keep.start()
        for t, i, rows, cols in tile_places(seq_len, heads, 0, seq_len):
            s_ref[i] = dot_nt(k_ref[tile_keys_of(t, span_keys), cols], q_ref[rows, cols])
        for low in (0, half):
            for t, i, rows, cols in tile_places(seq_len, heads, low, low + half):
                _, sg_ref[i] = weigh(s_ref[i], pg_ref[i], masks, t)
            for t, i, rows, cols in tile_places(seq_len, heads, low, low + half):
                k = k_ref[tile_keys_of(t, span_keys), cols]
                qg_ref[rows, cols] = (dot_tn(sg_ref[i], k) * scaling).astype(BF16)
            for b in range(low // BLOCK, (low + half) // BLOCK):
                rows = slice(b * BLOCK, (b + 1) * BLOCK)
                term_ref[rows, :] = dot_nt(qg_ref[rows, :], w_ref[...]).astype(BF16)
                store(b).start()
        for b in range(blocks):
            store(b).wait()
        keep.wait()

    return pl.pallas_call(
        kernel,
        out_shape=(
            pltpu.HBM((seq_len, mp_count * width), BF16),
            pltpu.HBM((seq_len, width), BF16),
        ),
        in_specs=[HBM, VMEM, VMEM, VMEM],
        out_specs=(HBM, HBM),
        scratch_shapes=[
            pltpu.VMEM((mp_count, seq_len, width), BF16),
            pltpu.VMEM((seq_len, mp_count * width), BF16),
            pltpu.VMEM((seq_len, width), BF16),
            pltpu.VMEM(prob_grads.shape, BF16),
            pltpu.VMEM((seq_len, width), BF16),
            pltpu.VMEM(prob_grads.shape, F32),
            pltpu.SemaphoreType.DMA((2,)),
            pltpu.SemaphoreType.DMA((blocks,)),
            pltpu.SemaphoreType.DMA(()),
        ],
        compiler_params=pltpu.CompilerParams(vmem_limit_bytes=24 * 1024 * 1024),
        name="attend",
    )(pltpu.with_memory_space_constraint(tokens, pltpu.HBM), q_weight, keys, prob_grads)


def finish(owners, queries, keys, values, prob_grads, cotangent, dp_count):
    seq_len, width = cotangent.shape
    heads = width // DH
    picks = owners.shape[0]
    span_keys = values.shape[0] // (seq_len // SPAN + 1)
    nei = span_keys // NEIGH
    tile_keys = prob_grads.shape[1]
    scaling = 1.0 / math.sqrt(DH)

    def kernel(
        own_ref, q_ref, k_ref, v_ref, pg_ref, cot_ref, att_ref, use_ref,
        s_ref, p_ref, sg_ref, ku_ref, vu_ref,
    ):
        use_ref[...] = jnp.zeros_like(use_ref)
        masks = attends(tile_keys, span_keys)
        for t, i, rows, cols in tile_places(seq_len, heads, 0, seq_len):
            s_ref[i] = dot_nt(k_ref[tile_keys_of(t, span_keys), cols], q_ref[rows, cols])
        for t, i, rows, cols in tile_places(seq_len, heads, 0, seq_len):
            p_ref[i], sg_ref[i] = weigh(s_ref[i], pg_ref[i], masks, t)
        for t, i, rows, cols in tile_places(seq_len, heads, 0, seq_len):
            keys_at = tile_keys_of(t, span_keys)
            start, mid, end = keys_at.start, keys_at.start + span_keys, keys_at.stop
            key_use = jnp.dot(sg_ref[i], q_ref[rows, cols], preferred_element_type=F32)
            value_use = jnp.dot(p_ref[i], cot_ref[rows, cols], preferred_element_type=F32)
            att_ref[rows, cols] = dot_tn(p_ref[i], v_ref[keys_at, cols]).astype(BF16)
            if t == 0:
                ku_ref[start:mid, cols] = key_use[:span_keys]
                vu_ref[start:mid, cols] = value_use[:span_keys]
            else:
                ku_ref[start:mid, cols] += key_use[:span_keys]
                vu_ref[start:mid, cols] += value_use[:span_keys]
            ku_ref[mid:end, cols] = key_use[span_keys:]
            vu_ref[mid:end, cols] = value_use[span_keys:]
        for n in range(picks):
            at = span_keys + n * nei
            use_ref[own_ref[n], :, :width] = (ku_ref[at : at + nei, :] * scaling).astype(BF16)
            use_ref[own_ref[n], :, width:] = vu_ref[at : at + nei, :].astype(BF16)

    return pl.pallas_call(
        kernel,
        out_shape=(
            jax.ShapeDtypeStruct((seq_len, width), BF16),
            jax.ShapeDtypeStruct((dp_count, nei, 2 * width), BF16),
        ),
        in_specs=[SMEM] + [VMEM] * 5,
        out_specs=(VMEM, VMEM),
        scratch_shapes=[
            pltpu.VMEM(prob_grads.shape, F32),
            pltpu.VMEM(prob_grads.shape, BF16),
            pltpu.VMEM(prob_grads.shape, BF16),
            pltpu.VMEM(values.shape, F32),
            pltpu.VMEM(values.shape, F32),
        ],
        compiler_params=pltpu.CompilerParams(vmem_limit_bytes=20 * 1024 * 1024),
        name="finish",
    )(owners, queries, keys, values, prob_grads, cotangent)


def body(
    tokens, q_weight, snippet_keys, snippet_values, out_cotangent, neighbour_ids, snippet_slot
):
    dp_count = lax.axis_size("dp")
    seq_len = tokens.shape[0]
    snip_count, nei, _ = snippet_keys.shape
    gathered = lax.all_gather(tokens, "mp", axis=0, tiled=False)
    request, owners = request_rows(neighbour_ids.T, snippet_slot, snip_count, dp_count)
    wanted = lax.all_to_all(request, "dp", split_axis=0, concat_axis=0, tiled=True)
    picked = pick_rows(wanted, snippet_keys, snippet_values)
    got = lax.all_to_all(picked, "dp", split_axis=0, concat_axis=0, tiled=True)
    values, keys, prob_grads = prepare(owners, out_cotangent, got)
    terms, queries = attend(
        gathered, q_weight, keys, prob_grads, seq_len, NEIGH * nei
    )
    input_grad = lax.psum_scatter(terms, "mp", scatter_dimension=1, tiled=True)
    attended, uses = finish(
        owners, queries, keys, values, prob_grads, out_cotangent, dp_count
    )
    back = lax.all_to_all(uses, "dp", split_axis=0, concat_axis=0, tiled=True)
    key_grad, value_grad = sum_uses(wanted, back, snip_count)
    return (attended, input_grad, key_grad, value_grad)


def solution(mesh):
    return jax.shard_map(
        body,
        mesh=mesh,
        in_specs=(
            P("dp", "mp"),
            P(None, "mp"),
            P("dp", None, "mp"),
            P("dp", None, "mp"),
            P("dp", "mp"),
            P("dp", None),
            P(),
        ),
        out_specs=(P("dp", "mp"), P("dp", "mp"), P("dp", None, "mp"), P("dp", None, "mp")),
        check_vma=False,
    )
```

```python
import math

import jax
import jax.numpy as jnp
from jax import lax
from jax.experimental import pallas as pl
from jax.experimental.pallas import tpu as pltpu
from jax.sharding import PartitionSpec as P

DH = 128
SPAN = 64
NEIGH = 2
TILE = 2 * SPAN
BLOCK = 2 * TILE
LANES = 128
F32 = jnp.float32
BF16 = jnp.bfloat16

VMEM = pl.BlockSpec(memory_space=pltpu.MemorySpace.VMEM)
SMEM = pl.BlockSpec(memory_space=pltpu.MemorySpace.SMEM)
HBM = pl.BlockSpec(memory_space=pltpu.MemorySpace.HBM)


def dot_nt(a, b):
    return lax.dot_general(a, b, (((1,), (1,)), ((), ())), preferred_element_type=F32)


def dot_tn(a, b):
    return lax.dot_general(a, b, (((0,), (0,)), ((), ())), preferred_element_type=F32)


def request_rows(ids, slot_table, snip_count, dp_count):
    spans = ids.shape[1]

    def kernel(ids_ref, slot_ref, req_ref, own_ref):
        def clear(i, c):
            req_ref[i, 0, 0] = 0
            return c

        lax.fori_loop(0, dp_count, clear, 0, unroll=16)

        def step(i, c):
            for n in range(NEIGH):
                slot = slot_ref[ids_ref[n, i]]
                owner = lax.div(slot, snip_count)
                req_ref[owner, 0, 0] = slot - owner * snip_count + 1
                own_ref[i * NEIGH + n] = owner
            return c

        lax.fori_loop(0, spans, step, 0, unroll=4)

    return pl.pallas_call(
        kernel,
        out_shape=(
            jax.ShapeDtypeStruct((dp_count, 1, LANES), jnp.int32),
            jax.ShapeDtypeStruct((spans * NEIGH,), jnp.int32),
        ),
        in_specs=[SMEM, SMEM],
        out_specs=(SMEM, SMEM),
        name="request_rows",
    )(ids, slot_table)


def pick_rows(wanted, keys, values):
    dp_count = wanted.shape[0]
    _, nei, width = keys.shape

    def kernel(want_ref, key_ref, value_ref, out_ref):
        def step(i, c):
            row = jnp.maximum(want_ref[i, 0, 0] - 1, 0)
            out_ref[i, :, :width] = key_ref[row]
            out_ref[i, :, width:] = value_ref[row]
            return c

        lax.fori_loop(0, dp_count, step, 0, unroll=4)

    return pl.pallas_call(
        kernel,
        out_shape=pltpu.VMEM((dp_count, nei, 2 * width), keys.dtype),
        in_specs=[SMEM, VMEM, VMEM],
        out_specs=VMEM,
        name="pick_rows",
    )(wanted, keys, values)


def sum_uses(wanted, back, snip_count):
    dp_count, nei, twice = back.shape
    width = twice // 2

    def kernel(want_ref, back_ref, key_ref, value_ref):
        key_ref[...] = jnp.zeros_like(key_ref)
        value_ref[...] = jnp.zeros_like(value_ref)

        def step(i, c):
            want = want_ref[i, 0, 0]

            @pl.when(want > 0)
            def _():
                row = jnp.maximum(want - 1, 0)
                key_ref[row] += back_ref[i, :, :width].astype(F32)
                value_ref[row] += back_ref[i, :, width:].astype(F32)

            return c

        lax.fori_loop(0, dp_count, step, 0)

    out = jax.ShapeDtypeStruct((snip_count, nei, width), F32)
    return pl.pallas_call(
        kernel,
        out_shape=(out, out),
        in_specs=[SMEM, VMEM],
        out_specs=(VMEM, VMEM),
        name="sum_uses",
    )(wanted, back)


def tile_keys_of(t, span_keys):
    start = t * (TILE // SPAN) * span_keys
    return slice(start, start + (TILE // SPAN + 1) * span_keys)


def prepare(owners, cotangent, got):
    seq_len, width = cotangent.shape
    nei = got.shape[1]
    heads = width // DH
    picks = owners.shape[0]
    span_keys = NEIGH * nei
    tiles = seq_len // TILE
    padded = (seq_len // SPAN + 1) * span_keys
    tile_keys = (TILE // SPAN + 1) * span_keys

    def kernel(own_ref, cot_ref, got_ref, v_ref, k_ref, pg_ref):
        k_ref[:span_keys, :] = jnp.zeros((span_keys, width), BF16)
        v_ref[:span_keys, :] = jnp.zeros((span_keys, width), BF16)
        for n in range(picks):
            at = span_keys + n * nei
            k_ref[at : at + nei, :] = got_ref[own_ref[n], :, :width]
            v_ref[at : at + nei, :] = got_ref[own_ref[n], :, width:]
        for t in range(tiles):
            rows = slice(t * TILE, (t + 1) * TILE)
            for h in range(heads):
                cols = slice(h * DH, (h + 1) * DH)
                pg_ref[t * heads + h] = dot_nt(v_ref[tile_keys_of(t, span_keys), cols], cot_ref[rows, cols])

    return pl.pallas_call(
        kernel,
        out_shape=(
            jax.ShapeDtypeStruct((padded, width), BF16),
            jax.ShapeDtypeStruct((padded, width), BF16),
            jax.ShapeDtypeStruct((tiles * heads, tile_keys, TILE), F32),
        ),
        in_specs=[SMEM, VMEM, VMEM],
        out_specs=(VMEM, VMEM, VMEM),
        compiler_params=pltpu.CompilerParams(vmem_limit_bytes=16 * 1024 * 1024),
        name="prepare",
    )(pltpu.with_memory_space_constraint(owners, pltpu.HBM), cotangent, got)


def tile_places(seq_len, heads, low, high):
    for t in range(low // TILE, high // TILE):
        for h in range(heads):
            yield t, t * heads + h, slice(t * TILE, (t + 1) * TILE), slice(h * DH, (h + 1) * DH)


def attends(tile_keys, span_keys):
    key_at = lax.broadcasted_iota(jnp.int32, (tile_keys, TILE), 0) // span_keys
    span_of = (lax.broadcasted_iota(jnp.int32, (tile_keys, TILE), 1) + 1) // SPAN
    inner = key_at == span_of
    return inner, inner & (key_at > 0)


def weigh(products, prob_grad, masks, t):
    scores = jnp.where(masks[0] if t else masks[1], products * (1.0 / math.sqrt(DH)), -jnp.inf)
    top = jnp.max(scores, axis=0, keepdims=True)
    if t == 0:
        top = jnp.where(top == -jnp.inf, 0.0, top)
    grown = jnp.exp(scores - top)
    total = jnp.sum(grown, axis=0, keepdims=True)
    if t == 0:
        total = jnp.where(total > 0.0, total, 1.0)
    weights = grown * (1.0 / total)
    row_delta = jnp.sum(weights * prob_grad, axis=0, keepdims=True)
    return weights.astype(BF16), (weights * (prob_grad - row_delta)).astype(BF16)


def attend(tokens, q_weight, keys, prob_grads, seq_len, span_keys):
    mp_count, given, width = tokens.shape
    heads = width // DH
    blocks = seq_len // BLOCK
    tile_keys = prob_grads.shape[1]
    scaling = 1.0 / math.sqrt(DH)
    skip = seq_len - given
    half = seq_len // 2

    def kernel(
        tok_hbm, w_ref, k_ref, pg_ref, term_hbm, q_hbm,
        tok_ref, term_ref, q_ref, sg_ref, qg_ref, s_ref, in_sem, out_sem, keep_sem,
    ):
        def load(i):
            low, high = (half, seq_len) if i else (skip, half)
            source = tok_hbm.at[:, low - skip : high - skip, :]
            return pltpu.make_async_copy(source, tok_ref.at[:, low:high, :], in_sem.at[i])

        def store(b):
            low, high = max(b * BLOCK, skip), (b + 1) * BLOCK
            target = term_hbm.at[low - skip : high - skip, :]
            return pltpu.make_async_copy(term_ref.at[low:high, :], target, out_sem.at[b])

        load(0).start()
        load(1).start()
        keep = pltpu.make_async_copy(q_ref, q_hbm, keep_sem)
        masks = attends(tile_keys, span_keys)
        q_ref[:skip, :] = jnp.zeros((skip, width), BF16)
        load(0).wait()
        for b in range(blocks):
            if b * BLOCK == half:
                load(1).wait()
            rows = slice(max(b * BLOCK, skip), (b + 1) * BLOCK)
            x = jnp.concatenate([tok_ref[j, rows, :] for j in range(mp_count)], axis=1)
            q_ref[rows, :] = jnp.dot(x, w_ref[...], preferred_element_type=F32).astype(BF16)
        keep.start()
        for t, i, rows, cols in tile_places(seq_len, heads, 0, seq_len):
            s_ref[i] = dot_nt(k_ref[tile_keys_of(t, span_keys), cols], q_ref[rows, cols])
        for low in (0, half):
            for t, i, rows, cols in tile_places(seq_len, heads, low, low + half):
                _, sg_ref[i] = weigh(s_ref[i], pg_ref[i], masks, t)
            for t, i, rows, cols in tile_places(seq_len, heads, low, low + half):
                k = k_ref[tile_keys_of(t, span_keys), cols]
                qg_ref[rows, cols] = (dot_tn(sg_ref[i], k) * scaling).astype(BF16)
            for b in range(low // BLOCK, (low + half) // BLOCK):
                rows = slice(max(b * BLOCK, skip), (b + 1) * BLOCK)
                term_ref[rows, :] = dot_nt(qg_ref[rows, :], w_ref[...]).astype(BF16)
                store(b).start()
        for b in range(blocks):
            store(b).wait()
        keep.wait()

    return pl.pallas_call(
        kernel,
        out_shape=(
            pltpu.HBM((given, mp_count * width), BF16),
            pltpu.HBM((seq_len, width), BF16),
        ),
        in_specs=[HBM, VMEM, VMEM, VMEM],
        out_specs=(HBM, HBM),
        scratch_shapes=[
            pltpu.VMEM((mp_count, seq_len, width), BF16),
            pltpu.VMEM((seq_len, mp_count * width), BF16),
            pltpu.VMEM((seq_len, width), BF16),
            pltpu.VMEM(prob_grads.shape, BF16),
            pltpu.VMEM((seq_len, width), BF16),
            pltpu.VMEM(prob_grads.shape, F32),
            pltpu.SemaphoreType.DMA((2,)),
            pltpu.SemaphoreType.DMA((blocks,)),
            pltpu.SemaphoreType.DMA(()),
        ],
        compiler_params=pltpu.CompilerParams(vmem_limit_bytes=24 * 1024 * 1024),
        name="attend",
    )(pltpu.with_memory_space_constraint(tokens, pltpu.HBM), q_weight, keys, prob_grads)


def finish(owners, queries, keys, values, prob_grads, cotangent, dp_count):
    seq_len, width = cotangent.shape
    heads = width // DH
    picks = owners.shape[0]
    span_keys = values.shape[0] // (seq_len // SPAN + 1)
    nei = span_keys // NEIGH
    tile_keys = prob_grads.shape[1]
    scaling = 1.0 / math.sqrt(DH)

    def kernel(
        own_ref, q_ref, k_ref, v_ref, pg_ref, cot_ref, att_ref, use_ref,
        s_ref, p_ref, sg_ref, ku_ref, vu_ref,
    ):
        use_ref[...] = jnp.zeros_like(use_ref)
        masks = attends(tile_keys, span_keys)
        for t, i, rows, cols in tile_places(seq_len, heads, 0, seq_len):
            s_ref[i] = dot_nt(k_ref[tile_keys_of(t, span_keys), cols], q_ref[rows, cols])
        for t, i, rows, cols in tile_places(seq_len, heads, 0, seq_len):
            p_ref[i], sg_ref[i] = weigh(s_ref[i], pg_ref[i], masks, t)
        for t, i, rows, cols in tile_places(seq_len, heads, 0, seq_len):
            keys_at = tile_keys_of(t, span_keys)
            start, mid, end = keys_at.start, keys_at.start + span_keys, keys_at.stop
            key_use = jnp.dot(sg_ref[i], q_ref[rows, cols], preferred_element_type=F32)
            value_use = jnp.dot(p_ref[i], cot_ref[rows, cols], preferred_element_type=F32)
            att_ref[rows, cols] = dot_tn(p_ref[i], v_ref[keys_at, cols]).astype(BF16)
            if t == 0:
                ku_ref[start:mid, cols] = key_use[:span_keys]
                vu_ref[start:mid, cols] = value_use[:span_keys]
            else:
                ku_ref[start:mid, cols] += key_use[:span_keys]
                vu_ref[start:mid, cols] += value_use[:span_keys]
            ku_ref[mid:end, cols] = key_use[span_keys:]
            vu_ref[mid:end, cols] = value_use[span_keys:]
        for n in range(picks):
            at = span_keys + n * nei
            use_ref[own_ref[n], :, :width] = (ku_ref[at : at + nei, :] * scaling).astype(BF16)
            use_ref[own_ref[n], :, width:] = vu_ref[at : at + nei, :].astype(BF16)

    return pl.pallas_call(
        kernel,
        out_shape=(
            jax.ShapeDtypeStruct((seq_len, width), BF16),
            jax.ShapeDtypeStruct((dp_count, nei, 2 * width), BF16),
        ),
        in_specs=[SMEM] + [VMEM] * 5,
        out_specs=(VMEM, VMEM),
        scratch_shapes=[
            pltpu.VMEM(prob_grads.shape, F32),
            pltpu.VMEM(prob_grads.shape, BF16),
            pltpu.VMEM(prob_grads.shape, BF16),
            pltpu.VMEM(values.shape, F32),
            pltpu.VMEM(values.shape, F32),
        ],
        compiler_params=pltpu.CompilerParams(vmem_limit_bytes=20 * 1024 * 1024),
        name="finish",
    )(owners, queries, keys, values, prob_grads, cotangent)


def body(
    tokens, q_weight, snippet_keys, snippet_values, out_cotangent, neighbour_ids, snippet_slot
):
    dp_count = lax.axis_size("dp")
    seq_len = tokens.shape[0]
    snip_count, nei, _ = snippet_keys.shape
    skip = (SPAN - 1) // 16 * 16
    gathered = lax.all_gather(tokens[skip:], "mp", axis=0, tiled=False)
    request, owners = request_rows(neighbour_ids.T, snippet_slot, snip_count, dp_count)
    wanted = lax.all_to_all(request, "dp", split_axis=0, concat_axis=0, tiled=True)
    picked = pick_rows(wanted, snippet_keys, snippet_values)
    got = lax.all_to_all(picked, "dp", split_axis=0, concat_axis=0, tiled=True)
    values, keys, prob_grads = prepare(owners, out_cotangent, got)
    terms, queries = attend(
        gathered, q_weight, keys, prob_grads, seq_len, NEIGH * nei
    )
    input_grad = lax.psum_scatter(terms, "mp", scatter_dimension=1, tiled=True)
    input_grad = jnp.pad(input_grad, ((skip, 0), (0, 0)))
    attended, uses = finish(
        owners, queries, keys, values, prob_grads, out_cotangent, dp_count
    )
    back = lax.all_to_all(uses, "dp", split_axis=0, concat_axis=0, tiled=True)
    key_grad, value_grad = sum_uses(wanted, back, snip_count)
    return (attended, input_grad, key_grad, value_grad)


def solution(mesh):
    return jax.shard_map(
        body,
        mesh=mesh,
        in_specs=(
            P("dp", "mp"),
            P(None, "mp"),
            P("dp", None, "mp"),
            P("dp", None, "mp"),
            P("dp", "mp"),
            P("dp", None),
            P(),
        ),
        out_specs=(P("dp", "mp"), P("dp", "mp"), P("dp", None, "mp"), P("dp", None, "mp")),
        check_vma=False,
    )
```

```python
import math

import jax
import jax.numpy as jnp
from jax import lax
from jax.experimental import pallas as pl
from jax.experimental.pallas import tpu as pltpu
from jax.sharding import PartitionSpec as P

DH = 128
SPAN = 64
NEIGH = 2
TILE = 2 * SPAN
BLOCK = 2 * TILE
LANES = 128
F32 = jnp.float32
BF16 = jnp.bfloat16

VMEM = pl.BlockSpec(memory_space=pltpu.MemorySpace.VMEM)
SMEM = pl.BlockSpec(memory_space=pltpu.MemorySpace.SMEM)
HBM = pl.BlockSpec(memory_space=pltpu.MemorySpace.HBM)


def dot_nt(a, b):
    return lax.dot_general(a, b, (((1,), (1,)), ((), ())), preferred_element_type=F32)


def dot_tn(a, b):
    return lax.dot_general(a, b, (((0,), (0,)), ((), ())), preferred_element_type=F32)


def request_rows(ids, slot_table, snip_count, dp_count):
    spans = ids.shape[1]

    def kernel(ids_ref, slot_ref, req_ref, own_ref):
        def clear(i, c):
            req_ref[i, 0, 0] = 0
            return c

        lax.fori_loop(0, dp_count, clear, 0, unroll=16)

        def step(i, c):
            for n in range(NEIGH):
                slot = slot_ref[ids_ref[n, i]]
                owner = lax.div(slot, snip_count)
                req_ref[owner, 0, 0] = slot - owner * snip_count + 1
                own_ref[i * NEIGH + n] = owner
            return c

        lax.fori_loop(0, spans, step, 0, unroll=4)

    return pl.pallas_call(
        kernel,
        out_shape=(
            jax.ShapeDtypeStruct((dp_count, 1, LANES), jnp.int32),
            jax.ShapeDtypeStruct((spans * NEIGH,), jnp.int32),
        ),
        in_specs=[SMEM, SMEM],
        out_specs=(SMEM, SMEM),
        name="request_rows",
    )(ids, slot_table)


def pick_rows(wanted, keys, values):
    dp_count = wanted.shape[0]
    _, nei, width = keys.shape

    def kernel(want_ref, key_ref, value_ref, out_ref):
        def step(i, c):
            row = jnp.maximum(want_ref[i, 0, 0] - 1, 0)
            out_ref[i, :, :width] = key_ref[row]
            out_ref[i, :, width:] = value_ref[row]
            return c

        lax.fori_loop(0, dp_count, step, 0, unroll=4)

    return pl.pallas_call(
        kernel,
        out_shape=pltpu.VMEM((dp_count, nei, 2 * width), keys.dtype),
        in_specs=[SMEM, VMEM, VMEM],
        out_specs=VMEM,
        name="pick_rows",
    )(wanted, keys, values)


def sum_uses(wanted, back, snip_count):
    dp_count, nei, twice = back.shape
    width = twice // 2

    def kernel(want_ref, back_ref, key_ref, value_ref):
        key_ref[...] = jnp.zeros_like(key_ref)
        value_ref[...] = jnp.zeros_like(value_ref)

        def step(i, c):
            want = want_ref[i, 0, 0]

            @pl.when(want > 0)
            def _():
                row = jnp.maximum(want - 1, 0)
                key_ref[row] += back_ref[i, :, :width].astype(F32)
                value_ref[row] += back_ref[i, :, width:].astype(F32)

            return c

        lax.fori_loop(0, dp_count, step, 0)

    out = jax.ShapeDtypeStruct((snip_count, nei, width), F32)
    return pl.pallas_call(
        kernel,
        out_shape=(out, out),
        in_specs=[SMEM, VMEM],
        out_specs=(VMEM, VMEM),
        name="sum_uses",
    )(wanted, back)


def tile_keys_of(t, span_keys):
    start = t * (TILE // SPAN) * span_keys
    return slice(start, start + (TILE // SPAN + 1) * span_keys)


def prepare(owners, cotangent, got):
    seq_len, width = cotangent.shape
    nei = got.shape[1]
    heads = width // DH
    picks = owners.shape[0]
    span_keys = NEIGH * nei
    tiles = seq_len // TILE
    padded = (seq_len // SPAN + 1) * span_keys
    tile_keys = (TILE // SPAN + 1) * span_keys

    def kernel(own_ref, cot_ref, got_ref, v_ref, k_ref, pg_ref):
        k_ref[:span_keys, :] = jnp.zeros((span_keys, width), BF16)
        v_ref[:span_keys, :] = jnp.zeros((span_keys, width), BF16)
        for n in range(picks):
            at = span_keys + n * nei
            k_ref[at : at + nei, :] = got_ref[own_ref[n], :, :width]
            v_ref[at : at + nei, :] = got_ref[own_ref[n], :, width:]
        for t in range(tiles):
            rows = slice(t * TILE, (t + 1) * TILE)
            for h in range(heads):
                cols = slice(h * DH, (h + 1) * DH)
                pg_ref[t * heads + h] = dot_nt(v_ref[tile_keys_of(t, span_keys), cols], cot_ref[rows, cols])

    return pl.pallas_call(
        kernel,
        out_shape=(
            jax.ShapeDtypeStruct((padded, width), BF16),
            jax.ShapeDtypeStruct((padded, width), BF16),
            jax.ShapeDtypeStruct((tiles * heads, tile_keys, TILE), F32),
        ),
        in_specs=[SMEM, VMEM, VMEM],
        out_specs=(VMEM, VMEM, VMEM),
        compiler_params=pltpu.CompilerParams(vmem_limit_bytes=16 * 1024 * 1024),
        name="prepare",
    )(pltpu.with_memory_space_constraint(owners, pltpu.HBM), cotangent, got)


def tile_places(seq_len, heads, low, high):
    for t in range(low // TILE, high // TILE):
        for h in range(heads):
            yield t, t * heads + h, slice(t * TILE, (t + 1) * TILE), slice(h * DH, (h + 1) * DH)


def attends(tile_keys, span_keys):
    key_at = lax.broadcasted_iota(jnp.int32, (tile_keys, TILE), 0) // span_keys
    span_of = (lax.broadcasted_iota(jnp.int32, (tile_keys, TILE), 1) + 1) // SPAN
    inner = key_at == span_of
    return inner, inner & (key_at > 0)


def weigh(products, prob_grad, masks, t):
    scores = jnp.where(masks[0] if t else masks[1], products * (1.0 / math.sqrt(DH)), -jnp.inf)
    top = jnp.max(scores, axis=0, keepdims=True)
    if t == 0:
        top = jnp.where(top == -jnp.inf, 0.0, top)
    grown = jnp.exp(scores - top)
    total = jnp.sum(grown, axis=0, keepdims=True)
    if t == 0:
        total = jnp.where(total > 0.0, total, 1.0)
    weights = grown * (1.0 / total)
    row_delta = jnp.sum(weights * prob_grad, axis=0, keepdims=True)
    return weights.astype(BF16), (weights * (prob_grad - row_delta)).astype(BF16)


def attend(tokens, q_weight, keys, prob_grads, seq_len, span_keys):
    mp_count, given, width = tokens.shape
    heads = width // DH
    blocks = seq_len // BLOCK
    tile_keys = prob_grads.shape[1]
    scaling = 1.0 / math.sqrt(DH)
    skip = seq_len - given
    half = seq_len // 2

    def kernel(
        tok_hbm, w_ref, k_ref, pg_ref, term_hbm, q_hbm,
        tok_ref, term_ref, q_ref, sg_ref, qg_ref, s_ref, in_sem, out_sem, keep_sem,
    ):
        def load(i):
            low, high = (half, seq_len) if i else (skip, half)
            source = tok_hbm.at[:, low - skip : high - skip, :]
            return pltpu.make_async_copy(source, tok_ref.at[:, low:high, :], in_sem.at[i])

        def store(b):
            rows = slice(b * BLOCK, (b + 1) * BLOCK)
            return pltpu.make_async_copy(term_ref.at[rows, :], term_hbm.at[rows, :], out_sem.at[b])

        load(0).start()
        load(1).start()
        keep = pltpu.make_async_copy(q_ref, q_hbm, keep_sem)
        masks = attends(tile_keys, span_keys)
        q_ref[:skip, :] = jnp.zeros((skip, width), BF16)
        load(0).wait()
        for b in range(blocks):
            if b * BLOCK == half:
                load(1).wait()
            rows = slice(max(b * BLOCK, skip), (b + 1) * BLOCK)
            x = jnp.concatenate([tok_ref[j, rows, :] for j in range(mp_count)], axis=1)
            q_ref[rows, :] = jnp.dot(x, w_ref[...], preferred_element_type=F32).astype(BF16)
        keep.start()
        for t, i, rows, cols in tile_places(seq_len, heads, 0, seq_len):
            s_ref[i] = dot_nt(k_ref[tile_keys_of(t, span_keys), cols], q_ref[rows, cols])
        for low in (0, half):
            for t, i, rows, cols in tile_places(seq_len, heads, low, low + half):
                _, sg_ref[i] = weigh(s_ref[i], pg_ref[i], masks, t)
            for t, i, rows, cols in tile_places(seq_len, heads, low, low + half):
                k = k_ref[tile_keys_of(t, span_keys), cols]
                qg_ref[rows, cols] = (dot_tn(sg_ref[i], k) * scaling).astype(BF16)
            for b in range(low // BLOCK, (low + half) // BLOCK):
                rows = slice(b * BLOCK, (b + 1) * BLOCK)
                term_ref[rows, :] = dot_nt(qg_ref[rows, :], w_ref[...]).astype(BF16)
                store(b).start()
        for b in range(blocks):
            store(b).wait()
        keep.wait()

    return pl.pallas_call(
        kernel,
        out_shape=(
            pltpu.HBM((seq_len, mp_count * width), BF16),
            pltpu.HBM((seq_len, width), BF16),
        ),
        in_specs=[HBM, VMEM, VMEM, VMEM],
        out_specs=(HBM, HBM),
        scratch_shapes=[
            pltpu.VMEM((mp_count, seq_len, width), BF16),
            pltpu.VMEM((seq_len, mp_count * width), BF16),
            pltpu.VMEM((seq_len, width), BF16),
            pltpu.VMEM(prob_grads.shape, BF16),
            pltpu.VMEM((seq_len, width), BF16),
            pltpu.VMEM(prob_grads.shape, F32),
            pltpu.SemaphoreType.DMA((2,)),
            pltpu.SemaphoreType.DMA((blocks,)),
            pltpu.SemaphoreType.DMA(()),
        ],
        compiler_params=pltpu.CompilerParams(vmem_limit_bytes=24 * 1024 * 1024),
        name="attend",
    )(pltpu.with_memory_space_constraint(tokens, pltpu.HBM), q_weight, keys, prob_grads)


def finish(owners, queries, keys, values, prob_grads, cotangent, dp_count):
    seq_len, width = cotangent.shape
    heads = width // DH
    picks = owners.shape[0]
    span_keys = values.shape[0] // (seq_len // SPAN + 1)
    nei = span_keys // NEIGH
    tile_keys = prob_grads.shape[1]
    scaling = 1.0 / math.sqrt(DH)

    def kernel(
        own_ref, q_ref, k_ref, v_ref, pg_ref, cot_ref, att_ref, use_ref,
        s_ref, p_ref, sg_ref, ku_ref, vu_ref,
    ):
        use_ref[...] = jnp.zeros_like(use_ref)
        masks = attends(tile_keys, span_keys)
        for t, i, rows, cols in tile_places(seq_len, heads, 0, seq_len):
            s_ref[i] = dot_nt(k_ref[tile_keys_of(t, span_keys), cols], q_ref[rows, cols])
        for t, i, rows, cols in tile_places(seq_len, heads, 0, seq_len):
            p_ref[i], sg_ref[i] = weigh(s_ref[i], pg_ref[i], masks, t)
        for t, i, rows, cols in tile_places(seq_len, heads, 0, seq_len):
            keys_at = tile_keys_of(t, span_keys)
            start, mid, end = keys_at.start, keys_at.start + span_keys, keys_at.stop
            key_use = jnp.dot(sg_ref[i], q_ref[rows, cols], preferred_element_type=F32)
            value_use = jnp.dot(p_ref[i], cot_ref[rows, cols], preferred_element_type=F32)
            att_ref[rows, cols] = dot_tn(p_ref[i], v_ref[keys_at, cols]).astype(BF16)
            if t == 0:
                ku_ref[start:mid, cols] = key_use[:span_keys]
                vu_ref[start:mid, cols] = value_use[:span_keys]
            else:
                ku_ref[start:mid, cols] += key_use[:span_keys]
                vu_ref[start:mid, cols] += value_use[:span_keys]
            ku_ref[mid:end, cols] = key_use[span_keys:]
            vu_ref[mid:end, cols] = value_use[span_keys:]
        for n in range(picks):
            at = span_keys + n * nei
            use_ref[own_ref[n], :, :width] = (ku_ref[at : at + nei, :] * scaling).astype(BF16)
            use_ref[own_ref[n], :, width:] = vu_ref[at : at + nei, :].astype(BF16)

    return pl.pallas_call(
        kernel,
        out_shape=(
            jax.ShapeDtypeStruct((seq_len, width), BF16),
            jax.ShapeDtypeStruct((dp_count, nei, 2 * width), BF16),
        ),
        in_specs=[SMEM] + [VMEM] * 5,
        out_specs=(VMEM, VMEM),
        scratch_shapes=[
            pltpu.VMEM(prob_grads.shape, F32),
            pltpu.VMEM(prob_grads.shape, BF16),
            pltpu.VMEM(prob_grads.shape, BF16),
            pltpu.VMEM(values.shape, F32),
            pltpu.VMEM(values.shape, F32),
        ],
        compiler_params=pltpu.CompilerParams(vmem_limit_bytes=20 * 1024 * 1024),
        name="finish",
    )(owners, queries, keys, values, prob_grads, cotangent)


def body(
    tokens, q_weight, snippet_keys, snippet_values, out_cotangent, neighbour_ids, snippet_slot
):
    dp_count = lax.axis_size("dp")
    seq_len = tokens.shape[0]
    snip_count, nei, _ = snippet_keys.shape
    skip = (SPAN - 1) // 16 * 16
    gathered = lax.all_gather(tokens[skip:], "mp", axis=0, tiled=False)
    request, owners = request_rows(neighbour_ids.T, snippet_slot, snip_count, dp_count)
    wanted = lax.all_to_all(request, "dp", split_axis=0, concat_axis=0, tiled=True)
    picked = pick_rows(wanted, snippet_keys, snippet_values)
    got = lax.all_to_all(picked, "dp", split_axis=0, concat_axis=0, tiled=True)
    values, keys, prob_grads = prepare(owners, out_cotangent, got)
    terms, queries = attend(
        gathered, q_weight, keys, prob_grads, seq_len, NEIGH * nei
    )
    input_grad = lax.psum_scatter(terms, "mp", scatter_dimension=1, tiled=True)
    attended, uses = finish(
        owners, queries, keys, values, prob_grads, out_cotangent, dp_count
    )
    back = lax.all_to_all(uses, "dp", split_axis=0, concat_axis=0, tiled=True)
    key_grad, value_grad = sum_uses(wanted, back, snip_count)
    return (attended, input_grad, key_grad, value_grad)


def solution(mesh):
    return jax.shard_map(
        body,
        mesh=mesh,
        in_specs=(
            P("dp", "mp"),
            P(None, "mp"),
            P("dp", None, "mp"),
            P("dp", None, "mp"),
            P("dp", "mp"),
            P("dp", None),
            P(),
        ),
        out_specs=(P("dp", "mp"), P("dp", "mp"), P("dp", None, "mp"), P("dp", None, "mp")),
        check_vma=False,
    )
```
